256 devices in a mesh: gx: 8 (over z), gy: 32 (over y, x, core).
Axes of the slice: x: 4, y: 4, z: 8, core: 2. Of those that a mesh axis runs over, the one named last changes fastest.
Arguments:
- child_coef: bfloat16 [512, 16, 128, 128], P(('gx', 'gy')), may hold values from -6 to 6
- transfer: bfloat16 [512, 64, 2, 128, 128], P(('gx', 'gy')), may hold values from -0.125 to 0.125
- child_dir: int32 [512, 64], P(('gx', 'gy')), may hold values from 0 to 15, as said below
- couple_src: int32 [64, 64, 7], P('gx', 'gy'), may hold values from 0 to 63, as said below
- couple_kind: int32 [64, 64, 7], P('gx', 'gy'), may hold values from 0 to 7
- couple_count: int32 [64, 64], P('gx', 'gy'), may hold values from 1 to 7, as said below
- couple_table: bfloat16 [64, 8, 2, 128, 128], P('gy'), may hold values from -0.1875 to 0.1875
Outputs:
- child_local: bfloat16 [512, 16, 128, 128], P(('gx', 'gy'))
The draws below stay inside these ranges and needn't reach their ends.
Inputs may be any that keep to these rules, and one draw needn't show every extreme that they name: `child_dir`: in every row each child direction is named by exactly four parent directions. `couple_src`: the entries of one block row are distinct and never the row's own parent cluster. `couple_count`: some row holds 7.
All inputs are finite; a program needn't handle non-finite values.
Results may differ from the reference program's by a relative error of at most 0.015.
Values may be sent and summed in bfloat16 or wider, within the bound.
A program may use at most 128 MiB of HBM per device.

```python
import jax
import jax.numpy as jnp
from jax import lax

R = 128
A = 64
CPD = 2
DP = 64
MAXC = 7
NOFF = 8
DC = 16
CLUSTERS = 512
PARENTS = 64


def draw_child_dir(key, part):
    subkeys = jax.random.split(key, CLUSTERS)

    def shuffle_one(subkey):
        return jax.random.permutation(subkey, DP)
    shuffled = jax.vmap(shuffle_one)(subkeys)
    return (shuffled % DC).astype(jnp.int32)


def draw_couple_src(key, part):
    subkeys = jax.random.split(key, PARENTS * DP)

    def pick_row(subkey):
        return jax.random.permutation(subkey, PARENTS - 1)[:MAXC]
    chosen = jax.vmap(pick_row)(subkeys).reshape((PARENTS, DP, MAXC)).astype(jnp.int32)
    own_row = jnp.arange(PARENTS, dtype=jnp.int32)[:, None, None]
    return jnp.where(chosen >= own_row, chosen + 1, chosen).astype(jnp.int32)


def draw_couple_count(key, part):
    counts = jax.random.randint(key, (PARENTS, DP), 1, MAXC + 1).astype(jnp.int32)
    return counts.at[0, 0].set(MAXC).astype(jnp.int32)


def touch_ends(entries, key, least, largest):
    index_at = [jax.random.randint(jax.random.fold_in(key, axis), (), 0, length) for axis, length in enumerate(entries.shape)]
    widest = entries.shape.index(max(entries.shape))
    beside = index_at[:widest] + [(index_at[widest] + 1) % entries.shape[widest]] + index_at[widest + 1:]
    return entries.at[tuple(index_at)].set(least).at[tuple(beside)].set(largest)


def block_levels(key, extent, shards, low, top_value):
    def one(dim, blocks):
        heights = jax.random.uniform(jax.random.fold_in(jax.random.fold_in(key, 6), dim), (blocks,), jnp.float32, low / len(shards), top_value / len(shards))
        return jnp.repeat(jnp.exp(heights), extent[dim] // blocks).reshape((-1,) + (1,) * (len(extent) - dim - 1))

    loudness = one(*shards[0])
    for cut in shards[1:]:
        loudness = loudness * one(*cut)
    return loudness


def scatter_about(own_key, dims, scale, bound, cuts=(), kind=jnp.bfloat16):
    drawn = jax.random.normal(own_key, dims, jnp.float32) * scale
    if len(cuts) > 0:
        drawn = block_levels(own_key, dims, cuts, -0.22, 0.18) * drawn
    return jnp.clip(drawn, min=-bound, max=bound).astype(kind)


def setup_inputs(seed: int = 0) -> dict:
    splits = jax.random.split(jax.random.key(seed), 8)
    child_coef = scatter_about(splits[0], (CLUSTERS, DC, R, 2 * A), 1.0, 6.0, ((0, 256),))
    transfer = scatter_about(splits[1], (CLUSTERS, DP, 2, R, R), (16 * R) ** -0.5, 0.125, ((0, 256),))
    child_dir = draw_child_dir(jax.random.fold_in(splits[7], 71), 0)
    couple_src = draw_couple_src(jax.random.fold_in(splits[7], 71), 0)
    couple_kind = touch_ends(jax.random.randint(splits[4], (PARENTS, DP, MAXC), 0, NOFF), jax.random.fold_in(splits[4], 1), 0, NOFF - 1).astype(jnp.int32)
    couple_count = draw_couple_count(jax.random.fold_in(splits[7], 71), 0)
    couple_table = scatter_about(splits[6], (DP, NOFF, 2, R, R), (R * (MAXC + 1)) ** -0.5, 0.1875, ((0, 32),))
    return dict(child_coef=child_coef, transfer=transfer, child_dir=child_dir, couple_src=couple_src, couple_kind=couple_kind, couple_count=couple_count, couple_table=couple_table)


def complex_apply(real_part, imag_part, vectors, pattern):
    halfway = vectors.shape[-1] // 2
    vectors = vectors.astype(jnp.float32)
    real_term = jnp.einsum(pattern, real_part.astype(jnp.float32), vectors, precision=lax.Precision.HIGHEST)
    imag_term = jnp.einsum(pattern, imag_part.astype(jnp.float32), vectors, precision=lax.Precision.HIGHEST)
    return jnp.concatenate([real_term[..., :halfway] - imag_term[..., halfway:], real_term[..., halfway:] + imag_term[..., :halfway]], axis=-1)


def reference(child_coef, transfer, child_dir, couple_src, couple_kind, couple_count, couple_table):
    coef_groups = child_coef.reshape((PARENTS, 8, DC, R, 2 * A))
    transfer_groups = transfer.reshape((PARENTS, 8, DP, 2, R, R))
    dir_groups = child_dir.reshape((PARENTS, 8, DP)).astype(jnp.int32)

    def ascend(inputs):
        coefs, matrices, directions = inputs
        picked = jnp.take_along_axis(coefs, directions[:, :, None, None], axis=1)
        up_term = complex_apply(matrices[:, :, 0], matrices[:, :, 1], picked, "kers,kesa->kera")
        grouped = up_term.reshape((8 // CPD, CPD, DP, R, 2 * A))
        group_sum = jnp.sum(grouped, axis=1).astype(jnp.bfloat16)
        return jnp.sum(group_sum.astype(jnp.float32), axis=0).astype(jnp.bfloat16)

    parent = lax.map(ascend, (coef_groups, transfer_groups, dir_groups))
    dir_index = jnp.arange(DP, dtype=jnp.int32)[:, None]
    slot_index = jnp.arange(MAXC, dtype=jnp.int32)[None, :]

    def couple(inputs):
        sources_row, kinds_row, counts_row = inputs
        sources = parent[sources_row.astype(jnp.int32), dir_index]
        matrices = couple_table[dir_index, kinds_row.astype(jnp.int32)]
        products = complex_apply(matrices[:, :, 0], matrices[:, :, 1], sources, "emrs,emsa->emra")
        active = slot_index < counts_row[:, None]
        return jnp.sum(jnp.where(active[:, :, None, None], products, 0.0), axis=1).astype(jnp.bfloat16)

    parent_local = lax.map(couple, (couple_src, couple_kind, couple_count))
    child_index = jnp.arange(DC, dtype=jnp.int32)

    def descend(inputs):
        matrices, directions, local_row = inputs
        products = complex_apply(matrices[:, :, 0], matrices[:, :, 1], local_row, "kesr,esa->kera")
        onehot = (directions[:, None, :] == child_index[None, :, None]).astype(jnp.float32)
        return jnp.einsum("kie,kera->kira", onehot, products, precision=lax.Precision.HIGHEST).astype(jnp.bfloat16)

    child_local = lax.map(descend, (transfer_groups, dir_groups, parent_local))
    return child_local.reshape((CLUSTERS, DC, R, 2 * A))
```

```python
import functools

import jax
import jax.numpy as jnp
from jax import lax
from jax.experimental import pallas as pl
from jax.experimental.pallas import tpu as pltpu
from jax.sharding import PartitionSpec as P

MESH = pl.DeviceIdType.MESH
NT = (((1,), (1,)), ((), ()))
BF = jnp.bfloat16
F32 = jnp.float32
ZERO_SLOT = 512


def combine(z):
    z = z.reshape(z.shape[0] // 16, 2, 8, 256)
    re, im = z[:, 0], z[:, 1]
    out_re = re[:, :, :128] - im[:, :, 128:]
    out_im = im[:, :, :128] + re[:, :, 128:]
    return jnp.concatenate([out_re[:, None], out_im[:, None]], axis=1)


def kernel(
    dir_s, dir_v, idx_v, coef, table, tr_hbm,
    out,
    tr, vc, send_own, recv_c, tx, recv_x, fw, ry_m, ry_o, rz, pz, zk, lo, qz, fd, plo,
    idx_all, idx_s, list_v, list_s,
    sem_ld, sem_sm,
    cs, cr, xs, xr, fs, fr, ys, yr, zs, zr, is_, ir,
    zbs, zbr, ybs, ybr, fbs, fbr, xbs, xbr, cbs, cbr,
):
    z = lax.axis_index("gx")
    g = lax.axis_index("gy")
    c = lax.rem(g, 2)
    x = lax.rem(lax.div(g, 2), 4)
    y = lax.div(g, 8)
    xp = x + 1 - 2 * lax.rem(x, 2)
    xn = 3 - x
    xf = 3 - xp
    xh = lax.div(x, 2)
    oc = 1 - c

    def gid(yy, xx, cc):
        return (yy * 4 + xx) * 2 + cc

    dev_core = (z, gid(y, x, oc))
    dev_xp = (z, gid(y, xp, c))
    dev_xn = (z, gid(y, xn, c))

    def yo(dy):
        return lax.rem(y + dy, 4)

    def zo(dz):
        return lax.rem(z + dz, 8)

    def dev_y(yy):
        return (z, gid(yy, x, c))

    def dev_z(zz):
        return (zz, g)

    def rc(src, dst, ss, rs, dev):
        return pltpu.make_async_remote_copy(
            src_ref=src, dst_ref=dst, send_sem=ss, recv_sem=rs, device_id=dev, device_id_type=MESH
        )

    pend = []

    def go(cp):
        cp.start()
        pend.append(cp)

    YS = (2, 1, 3)
    ZS = (4, 3, 5, 2, 6, 1, 7)
    pri = (xf, xp, xn, x)

    barrier = pltpu.get_barrier_semaphore()
    partners = [dev_core, dev_xp, dev_xn] + [dev_y(yo(dy)) for dy in YS] + [dev_z(zo(dz)) for dz in ZS]
    for dev in partners:
        pl.semaphore_signal(barrier, inc=1, device_id=dev, device_id_type=MESH)

    loads = []
    for k in range(4):
        cp = pltpu.make_async_copy(tr_hbm.at[:, :, pri[k]], tr.at[:, :, pri[k]], sem_ld.at[k])
        cp.start()
        loads.append(cp)

    def prep(n, carry):
        cc = lax.div(n, 16)
        i = lax.rem(n, 16)
        vt = coef[cc, i].astype(F32).T.reshape(2, 8, 8, 128)
        v = jnp.concatenate([vt[0][:, None], vt[1][:, None]], axis=1)
        vc[cc, i] = v.reshape(128, 128).astype(BF)
        return carry

    lax.fori_loop(0, 32, prep, 0, unroll=2)

    pl.semaphore_wait(barrier, len(partners))

    for dz in ZS:
        go(rc(idx_v, idx_all.at[z], is_.at[zo(dz)], ir.at[z], dev_z(zo(dz))))
    idx_all[z] = idx_v[...]

    def up(d, k):
        def one(n, carry):
            yy = lax.rem(n, 4)
            first = lax.div(n, 4)
            cc = lax.rem(oc + first, 2)
            cd = cc * 2 + d
            e = yy * 16 + pri[k] * 4 + cd
            lhs = jnp.concatenate([vc[0, dir_s[0, e]], vc[1, dir_s[0, 64 + e]]], axis=1)
            rhs = jnp.concatenate(
                [tr[0, yy, pri[k], cd].reshape(256, 128), tr[1, yy, pri[k], cd].reshape(256, 128)], axis=1
            )
            r = combine(lax.dot_general(lhs, rhs, NT, preferred_element_type=F32))
            send_own[d, k, first, yy] = r.reshape(8, 16, 128).astype(BF)
            return carry

        lax.fori_loop(0, 8, one, 0, unroll=2)


    def core_send(d, k):
        go(rc(send_own.at[d, k, 0], recv_c.at[d, k], cs.at[d, k], cr.at[d, k], dev_core))

    def core_wait(d, k):
        rc(send_own.at[d, k, 0], recv_c.at[d, k], cs.at[d, k], cr.at[d, k], dev_core).wait_recv()

    def t_step(d, k):
        core_wait(d, k)
        for yy in range(4):
            tx[d, k, yy] = (send_own[d, k, 1, yy].astype(F32) + recv_c[d, k, yy].astype(F32)).astype(BF)
        go(rc(tx.at[d, k], recv_x.at[d, k], xs.at[d, k], xr.at[d, k], dev_xp))

    def x_wait(d, k):
        rc(tx.at[d, k], recv_x.at[d, k], xs.at[d, k], xr.at[d, k], dev_xp).wait_recv()

    def add3(d, k, yy):
        return (
            send_own[d, k + 2, 1, yy].astype(F32)
            + recv_c[d, k + 2, yy].astype(F32)
            + recv_x[d, k, yy].astype(F32)
        ).astype(BF)

    def f_step(d):
        core_wait(d, 2)
        x_wait(d, 0)
        for yy in range(4):
            fw[d, yy] = add3(d, 0, yy)
        go(rc(fw.at[d], ry_o.at[d], fs.at[d], fr.at[d], dev_xn))

    def y_copy(d, kind, src, yy):
        p = y * 2 + (xh if kind == 0 else 1 - xh)
        return rc(src.at[d, yy], rz.at[d, p], ys.at[d, kind, yy], yr.at[d, kind, y], dev_y(yy))

    def g_step(d):
        core_wait(d, 3)
        x_wait(d, 1)
        for yy in range(4):
            ry_m[d, yy] = add3(d, 1, yy)
        for dy in YS:
            go(y_copy(d, 0, ry_m, yo(dy)))
        rz[d, y * 2 + xh] = ry_m[d, y]

    def h_step(d):
        rc(fw.at[d], ry_o.at[d], fs.at[d], fr.at[d], dev_xn).wait_recv()
        for dy in YS:
            go(y_copy(d, 1, ry_o, yo(dy)))
        rz[d, y * 2 + 1 - xh] = ry_o[d, y]

    def z_send(d):
        for kind in range(2):
            for dy in YS:
                yy = yo(dy)
                p = yy * 2 + (xh if kind == 0 else 1 - xh)
                rc(ry_m.at[d, yy], rz.at[d, p], ys.at[d, kind, yy], yr.at[d, kind, yy], dev_y(yy)).wait_recv()
        for dz in ZS:
            zz = zo(dz)
            go(rc(rz.at[d, :, zz], pz.at[d, z], zs.at[d, zz], zr.at[d, z], dev_z(zz)))
        pz[d, z] = rz[d, :, z]

    order = [(d, k) for d in range(2) for k in range(4)]
    for n, (d, k) in enumerate(order):
        if d == 0:
            loads[k].wait()
        up(d, k)
        core_send(d, k)
        if n >= 1:
            pd, pk = order[n - 1]
            if pk < 2:
                t_step(pd, pk)

    row = jnp.broadcast_to(dir_v[...], (128, 128))
    lane = lax.broadcasted_iota(jnp.int32, (128, 128), 1)
    sub = lax.broadcasted_iota(jnp.int32, (128, 128), 0)
    row = row + jnp.where(lane >= 64, 16, 0)
    same = jnp.where((row == row.T) & (sub < lane), 1, 0)
    key = row * 4 + jnp.broadcast_to(jnp.sum(same, axis=0, keepdims=True), (128, 128))
    lst = jnp.sum(jnp.where(key.T == lane, sub, 0), axis=0, keepdims=True)
    list_v[...] = jnp.broadcast_to(lst, (8, 128))
    zk[ZERO_SLOT] = jnp.zeros((16, 128), F32)

    f_step(0)
    cp_list = pltpu.make_async_copy(list_v, list_s, sem_sm.at[0])
    cp_list.start()
    g_step(0)
    h_step(0)
    f_step(1)
    z_send(0)
    g_step(1)
    h_step(1)
    cp_list.wait()
    for dz in ZS:
        zz = zo(dz)
        rc(idx_v, idx_all.at[zz], is_.at[zz], ir.at[zz], dev_z(zz)).wait_recv()
    cp_idx = pltpu.make_async_copy(idx_all, idx_s, sem_sm.at[1])
    cp_idx.start()
    z_send(1)
    cp_idx.wait()

    def couple(d):
        for dz in ZS:
            zz = zo(dz)
            rc(rz.at[d, :, zz], pz.at[d, zz], zs.at[d, zz], zr.at[d, zz], dev_z(zz)).wait_recv()

        def dense(n, carry):
            k = lax.div(n, 4)
            q = lax.rem(n, 4)
            lhs = pz[d, pl.ds(q * 2, 2)].reshape(256, 128)
            r = combine(
                lax.dot_general(lhs, table[d, k].reshape(256, 128), NT, preferred_element_type=F32)
            )
            zk[pl.ds(n * 16, 16)] = r.reshape(16, 16, 128)
            return carry

        lax.fori_loop(0, 32, dense, 0)
        for dz in ZS + (0,):
            zz = zo(dz)

            def row_sum(p, carry):
                acc = zk[idx_s[zz, p, d * 8]]
                for m in range(1, 7):
                    acc = acc + zk[idx_s[zz, p, d * 8 + m]]
                lo[d, zz, p] = acc.astype(BF)
                return carry

            lax.fori_loop(0, 8, row_sum, 0, unroll=2)
            if dz:
                go(rc(lo.at[d, zz], qz.at[d, :, z], zbs.at[d, zz], zbr.at[d, z], dev_z(zz)))
        qz[d, :, z] = lo[d, z]

    def yb_step(d):
        for dz in ZS:
            zz = zo(dz)
            rc(lo.at[d, zz], qz.at[d, :, zz], zbs.at[d, zz], zbr.at[d, zz], dev_z(zz)).wait_recv()
        for dy in YS:
            yy = yo(dy)
            go(rc(qz.at[d, yy * 2 + 1 - xh], fd.at[d, y], ybs.at[d, 1, yy], ybr.at[d, 1, y], dev_y(yy)))
        for dy in YS:
            yy = yo(dy)
            go(rc(qz.at[d, yy * 2 + xh], plo.at[y, x, c * 2 + d], ybs.at[d, 0, yy], ybr.at[d, 0, y], dev_y(yy)))
        fd[d, y] = qz[d, y * 2 + 1 - xh]
        plo[y, x, c * 2 + d] = qz[d, y * 2 + xh]

    def grp(xx, cc, d):
        return plo.at[:, xx, cc * 2 + d]

    def cb_send(d, n, xx):
        go(rc(grp(xx, c, d), grp(xx, c, d), cbs.at[d, n], cbr.at[d, n], dev_core))

    cb_groups = (x, xn, xp, xf)

    def xb_step(d):
        for dy in YS:
            yy = yo(dy)
            rc(qz.at[d, yy * 2 + 1 - xh], fd.at[d, yy], ybs.at[d, 1, yy], ybr.at[d, 1, yy], dev_y(yy)).wait_recv()
        go(rc(fd.at[d], grp(x, c, d), fbs.at[d], fbr.at[d], dev_xn))
        for dy in YS:
            yy = yo(dy)
            rc(qz.at[d, yy * 2 + xh], plo.at[yy, x, c * 2 + d], ybs.at[d, 0, yy], ybr.at[d, 0, yy], dev_y(yy)).wait_recv()
        go(rc(grp(x, c, d), grp(x, c, d), xbs.at[d, 0], xbr.at[d, 0], dev_xp))
        cb_send(d, 0, x)

    def xb2_step(d):
        rc(fd.at[d], grp(xn, c, d), fbs.at[d], fbr.at[d], dev_xn).wait_recv()
        go(rc(grp(xn, c, d), grp(xn, c, d), xbs.at[d, 1], xbr.at[d, 1], dev_xp))
        cb_send(d, 1, xn)

    def xb3_step(d):
        rc(grp(x, c, d), grp(xp, c, d), xbs.at[d, 0], xbr.at[d, 0], dev_xp).wait_recv()
        cb_send(d, 2, xp)
        rc(grp(xn, c, d), grp(xf, c, d), xbs.at[d, 1], xbr.at[d, 1], dev_xp).wait_recv()
        cb_send(d, 3, xf)

    couple(0)
    couple(1)
    yb_step(0)
    xb_step(0)
    yb_step(1)
    xb2_step(0)
    xb3_step(0)
    xb_step(1)
    xb2_step(1)
    xb3_step(1)
    for d in range(2):
        for n in range(4):
            rc(grp(cb_groups[n], oc, d), grp(cb_groups[n], oc, d), cbs.at[d, n], cbr.at[d, n], dev_core).wait_recv()

    def down(n, carry):
        cc = lax.div(n, 16)
        i = lax.rem(n, 16)
        lhs, rhs = [], []
        for j in range(4):
            e = list_s[0, n * 4 + j] - cc * 64
            ey = lax.div(e, 16)
            ex = lax.rem(lax.div(e, 4), 4)
            ec = lax.rem(e, 4)
            lhs.append(plo[ey, ex, ec].reshape(128, 128))
            m = tr[cc, ey, ex, ec]
            rhs.append(jnp.concatenate([m[0], m[1]], axis=1))
        r = combine(
            jnp.dot(
                jnp.concatenate(lhs, axis=1), jnp.concatenate(rhs, axis=0), preferred_element_type=F32
            )
        )
        t = jnp.concatenate([r[:, 0].reshape(64, 128), r[:, 1].reshape(64, 128)], axis=0)
        out[cc, i] = t.T.astype(BF)
        return carry

    lax.fori_loop(0, 32, down, 0, unroll=2)
    for cp in pend:
        cp.wait_send()


def body(child_coef, transfer, child_dir, couple_src, couple_kind, couple_count, couple_table):
    dirs = child_dir.reshape(1, 128)
    active = jnp.arange(7, dtype=jnp.int32) < couple_count[..., None]
    idx = jnp.where(active, couple_kind * 64 + couple_src, ZERO_SLOT)
    idx = jnp.pad(idx, ((0, 0), (0, 0), (0, 1))).reshape(8, 16)
    idx = jnp.pad(idx, ((0, 0), (0, 112)))
    tr = transfer.reshape(2, 4, 4, 4, 2, 128, 128)
    vm = pl.BlockSpec(memory_space=pltpu.VMEM)
    dma = pltpu.SemaphoreType.DMA

    def blk(*lead):
        return pltpu.VMEM(lead + (8, 16, 128), BF)

    return pl.pallas_call(
        kernel,
        out_shape=jax.ShapeDtypeStruct((2, 16, 128, 128), BF),
        in_specs=[
            pl.BlockSpec(memory_space=pltpu.SMEM), vm, vm, vm, vm, pl.BlockSpec(memory_space=pl.ANY),
        ],
        out_specs=vm,
        scratch_shapes=[
            pltpu.VMEM((2, 4, 4, 4, 2, 128, 128), BF),
            pltpu.VMEM((2, 16, 128, 128), BF),
            blk(2, 4, 2, 4),
            blk(2, 4, 4),
            blk(2, 2, 4),
            blk(2, 2, 4),
            blk(2, 4),
            blk(2, 4),
            blk(2, 4),
            blk(2, 8),
            pltpu.VMEM((2, 8, 8, 16, 128), BF),
            pltpu.VMEM((ZERO_SLOT + 1, 16, 128), F32),
            pltpu.VMEM((2, 8, 8, 16, 128), BF),
            blk(2, 8),
            blk(2, 4),
            blk(4, 4, 4),
            pltpu.VMEM((8, 8, 128), jnp.int32),
            pltpu.SMEM((8, 8, 128), jnp.int32),
            pltpu.VMEM((8, 128), jnp.int32),
            pltpu.SMEM((8, 128), jnp.int32),
            dma((4,)), dma((2,)),
            dma((2, 4)), dma((2, 4)),
            dma((2, 2)), dma((2, 2)),
            dma((2,)), dma((2,)),
            dma((2, 2, 4)), dma((2, 2, 4)),
            dma((2, 8)), dma((2, 8)),
            dma((8,)), dma((8,)),
            dma((2, 8)), dma((2, 8)),
            dma((2, 2, 4)), dma((2, 2, 4)),
            dma((2,)), dma((2,)),
            dma((2, 2)), dma((2, 2)),
            dma((2, 4)), dma((2, 4)),
        ],
        compiler_params=pltpu.CompilerParams(
            collective_id=0, has_side_effects=True, vmem_limit_bytes=56 * 1024 * 1024
        ),
        name="h2_pass",
    )(dirs, dirs, idx, child_coef, couple_table, tr)


def solution(mesh):
    return jax.shard_map(
        body,
        mesh=mesh,
        in_specs=(
            P(("gx", "gy"), None, None, None),
            P(("gx", "gy"), None, None, None, None),
            P(("gx", "gy"), None),
            P("gx", "gy", None),
            P("gx", "gy", None),
            P("gx", "gy"),
            P("gy", None, None, None, None),
        ),
        out_specs=P(("gx", "gy"), None, None, None),
        check_vma=False,
    )
```

```python
import functools

import jax
import jax.numpy as jnp
from jax import lax
from jax.experimental import pallas as pl
from jax.experimental.pallas import tpu as pltpu
from jax.sharding import PartitionSpec as P

MESH = pl.DeviceIdType.MESH
NT = (((1,), (1,)), ((), ()))
BF = jnp.bfloat16
F32 = jnp.float32
ZERO_SLOT = 512


def combine(z):
    z = z.reshape(z.shape[0] // 16, 2, 8, 256)
    re, im = z[:, 0], z[:, 1]
    out_re = re[:, :, :128] - im[:, :, 128:]
    out_im = im[:, :, :128] + re[:, :, 128:]
    return jnp.concatenate([out_re[:, None], out_im[:, None]], axis=1)


def kernel(
    dir_s, dir_v, src_v, kind_v, count_v, coef_hbm, table_hbm, tr_hbm,
    out,
    coef, table, tr, vc, send_own, recv_c, tx, recv_x, fw, ry_m, ry_o, rz, pz, zk, lo, qz, fd, plo,
    idx_v, idx_all, idx_s, list_v, list_s,
    sem_ld, sem_sm,
    cs, cr, xs, xr, fs, fr, ys, yr, zs, zr, is_, ir,
    zbs, zbr, ybs, ybr, fbs, fbr, xbs, xbr, cbs, cbr,
):
    z = lax.axis_index("gx")
    g = lax.axis_index("gy")
    c = lax.rem(g, 2)
    x = lax.rem(lax.div(g, 2), 4)
    y = lax.div(g, 8)
    xp = x + 1 - 2 * lax.rem(x, 2)
    xn = 3 - x
    xf = 3 - xp
    xh = lax.div(x, 2)
    oc = 1 - c

    def gid(yy, xx, cc):
        return (yy * 4 + xx) * 2 + cc

    dev_core = (z, gid(y, x, oc))
    dev_xp = (z, gid(y, xp, c))
    dev_xn = (z, gid(y, xn, c))

    def yo(dy):
        return lax.rem(y + dy, 4)

    def zo(dz):
        return lax.rem(z + dz, 8)

    def dev_y(yy):
        return (z, gid(yy, x, c))

    def dev_z(zz):
        return (zz, g)

    def rc(src, dst, ss, rs, dev):
        return pltpu.make_async_remote_copy(
            src_ref=src, dst_ref=dst, send_sem=ss, recv_sem=rs, device_id=dev, device_id_type=MESH
        )

    pend = []

    def go(cp):
        cp.start()
        pend.append(cp)

    YS = (2, 1, 3)
    ZS = (4, 3, 5, 2, 6, 1, 7)
    pri = (xf, xp, xn, x)

    barrier = pltpu.get_barrier_semaphore()
    partners = [dev_core, dev_xp, dev_xn] + [dev_y(yo(dy)) for dy in YS] + [dev_z(zo(dz)) for dz in ZS]
    for dev in partners:
        pl.semaphore_signal(barrier, inc=1, device_id=dev, device_id_type=MESH)

    cp_coef = pltpu.make_async_copy(coef_hbm, coef, sem_ld.at[4])
    cp_coef.start()
    loads = []
    for k in range(4):
        cp = pltpu.make_async_copy(tr_hbm.at[:, :, pri[k]], tr.at[:, :, pri[k]], sem_ld.at[k])
        cp.start()
        loads.append(cp)

    cp_table = pltpu.make_async_copy(table_hbm, table, sem_ld.at[5])
    cp_table.start()

    for m in range(7):
        idx_v[2 * m : 2 * m + 2, 0:8] = jnp.where(
            count_v[...] > m, kind_v[m] * 64 + src_v[m], ZERO_SLOT
        )
    cp_coef.wait()

    def prep(n, carry):
        cc = lax.div(n, 16)
        i = lax.rem(n, 16)
        vt = coef[cc, i].astype(F32).T.reshape(2, 8, 8, 128)
        v = jnp.concatenate([vt[0][:, None], vt[1][:, None]], axis=1)
        vc[cc, i] = v.reshape(128, 128).astype(BF)
        return carry

    lax.fori_loop(0, 32, prep, 0, unroll=4)

    pl.semaphore_wait(barrier, len(partners))

    for dz in ZS:
        go(rc(idx_v, idx_all.at[z], is_.at[zo(dz)], ir.at[z], dev_z(zo(dz))))
    idx_all[z] = idx_v[...]

    def up(d, k):
        def one(n, carry):
            yy = lax.rem(n, 4)
            first = lax.div(n, 4)
            cc = lax.rem(oc + first, 2)
            cd = cc * 2 + d
            e = yy * 16 + pri[k] * 4 + cd
            lhs = jnp.concatenate([vc[0, dir_s[0, e]], vc[1, dir_s[1, e]]], axis=1)
            rhs = jnp.concatenate(
                [tr[0, yy, pri[k], cd].reshape(256, 128), tr[1, yy, pri[k], cd].reshape(256, 128)], axis=1
            )
            r = combine(lax.dot_general(lhs, rhs, NT, preferred_element_type=F32))
            send_own[d, k, first, yy] = r.reshape(8, 16, 128).astype(BF)
            return carry

        lax.fori_loop(0, 8, one, 0, unroll=8)


    def core_send(d, k):
        go(rc(send_own.at[d, k, 0], recv_c.at[d, k], cs.at[d, k], cr.at[d, k], dev_core))

    def core_wait(d, k):
        rc(send_own.at[d, k, 0], recv_c.at[d, k], cs.at[d, k], cr.at[d, k], dev_core).wait_recv()

    def t_step(d, k):
        core_wait(d, k)
        for yy in range(4):
            tx[d, k, yy] = (send_own[d, k, 1, yy].astype(F32) + recv_c[d, k, yy].astype(F32)).astype(BF)
        go(rc(tx.at[d, k], recv_x.at[d, k], xs.at[d, k], xr.at[d, k], dev_xp))

    def x_wait(d, k):
        rc(tx.at[d, k], recv_x.at[d, k], xs.at[d, k], xr.at[d, k], dev_xp).wait_recv()

    def add3(d, k, yy):
        return (
            send_own[d, k + 2, 1, yy].astype(F32)
            + recv_c[d, k + 2, yy].astype(F32)
            + recv_x[d, k, yy].astype(F32)
        ).astype(BF)

    def f_step(d):
        core_wait(d, 2)
        x_wait(d, 0)
        for yy in range(4):
            fw[d, yy] = add3(d, 0, yy)
        go(rc(fw.at[d], ry_o.at[d], fs.at[d], fr.at[d], dev_xn))

    def y_copy(d, kind, src, yy):
        p = y * 2 + (xh if kind == 0 else 1 - xh)
        return rc(src.at[d, yy], rz.at[d, p], ys.at[d, kind, yy], yr.at[d, kind, y], dev_y(yy))

    def g_step(d):
        core_wait(d, 3)
        x_wait(d, 1)
        for yy in range(4):
            ry_m[d, yy] = add3(d, 1, yy)
        for dy in YS:
            go(y_copy(d, 0, ry_m, yo(dy)))
        rz[d, y * 2 + xh] = ry_m[d, y]

    def h_step(d):
        rc(fw.at[d], ry_o.at[d], fs.at[d], fr.at[d], dev_xn).wait_recv()
        for dy in YS:
            go(y_copy(d, 1, ry_o, yo(dy)))
        rz[d, y * 2 + 1 - xh] = ry_o[d, y]

    def z_send(d):
        for kind in range(2):
            for dy in YS:
                yy = yo(dy)
                p = yy * 2 + (xh if kind == 0 else 1 - xh)
                rc(ry_m.at[d, yy], rz.at[d, p], ys.at[d, kind, yy], yr.at[d, kind, yy], dev_y(yy)).wait_recv()
        for dz in ZS:
            zz = zo(dz)
            go(rc(rz.at[d, :, zz], pz.at[d, z], zs.at[d, zz], zr.at[d, z], dev_z(zz)))
        pz[d, z] = rz[d, :, z]

    order = [(d, k) for d in range(2) for k in range(4)]
    for n, (d, k) in enumerate(order):
        if d == 0:
            loads[k].wait()
        up(d, k)
        core_send(d, k)
        if n >= 1:
            pd, pk = order[n - 1]
            if pk < 2:
                t_step(pd, pk)

    lane = lax.broadcasted_iota(jnp.int32, (128, 128), 1)
    sub = lax.broadcasted_iota(jnp.int32, (128, 128), 0)
    for cc in range(2):
        list_v[cc : cc + 1, 0:64] = dir_v[cc : cc + 1, :]
        row = jnp.where(lane < 64, jnp.broadcast_to(list_v[cc : cc + 1, :], (128, 128)), 64)
        same = jnp.where((row == row.T) & (sub < lane), 1, 0)
        key = row * 4 + jnp.broadcast_to(jnp.sum(same, axis=0, keepdims=True), (128, 128))
        list_v[cc : cc + 1, :] = jnp.sum(jnp.where(key.T == lane, sub, 0), axis=0, keepdims=True)
    zk[ZERO_SLOT] = jnp.zeros((16, 128), F32)

    f_step(0)
    cp_list = pltpu.make_async_copy(list_v, list_s, sem_sm.at[0])
    cp_list.start()
    g_step(0)
    h_step(0)
    f_step(1)
    z_send(0)
    g_step(1)
    h_step(1)
    cp_list.wait()
    for dz in ZS:
        zz = zo(dz)
        rc(idx_v, idx_all.at[zz], is_.at[zz], ir.at[zz], dev_z(zz)).wait_recv()
    cp_idx = pltpu.make_async_copy(idx_all, idx_s, sem_sm.at[1])
    cp_idx.start()
    z_send(1)
    cp_idx.wait()
    cp_table.wait()

    def couple(d):
        for dz in ZS:
            zz = zo(dz)
            rc(rz.at[d, :, zz], pz.at[d, zz], zs.at[d, zz], zr.at[d, zz], dev_z(zz)).wait_recv()

        def dense(k, carry):
            rhs = table[d, k].reshape(256, 128)
            for q in range(4):
                lhs = pz[d, q * 2 : q * 2 + 2].reshape(256, 128)
                r = combine(lax.dot_general(lhs, rhs, NT, preferred_element_type=F32))
                zk[pl.ds(k * 64 + q * 16, 16)] = r.reshape(16, 16, 128)
            return carry

        lax.fori_loop(0, 8, dense, 0, unroll=2)
        for dz in ZS + (0,):
            zz = zo(dz)

            def row_sum(p, carry):
                acc = zk[idx_s[zz, d, p]]
                for m in range(1, 7):
                    acc = acc + zk[idx_s[zz, 2 * m + d, p]]
                lo[d, zz, p] = acc.astype(BF)
                return carry

            lax.fori_loop(0, 8, row_sum, 0, unroll=4)
            if dz:
                go(rc(lo.at[d, zz], qz.at[d, :, z], zbs.at[d, zz], zbr.at[d, z], dev_z(zz)))
        qz[d, :, z] = lo[d, z]

    def yb_step(d):
        for dz in ZS:
            zz = zo(dz)
            rc(lo.at[d, zz], qz.at[d, :, zz], zbs.at[d, zz], zbr.at[d, zz], dev_z(zz)).wait_recv()
        for dy in YS:
            yy = yo(dy)
            go(rc(qz.at[d, yy * 2 + 1 - xh], fd.at[d, y], ybs.at[d, 1, yy], ybr.at[d, 1, y], dev_y(yy)))
        for dy in YS:
            yy = yo(dy)
            go(rc(qz.at[d, yy * 2 + xh], plo.at[y, x, c * 2 + d], ybs.at[d, 0, yy], ybr.at[d, 0, y], dev_y(yy)))
        fd[d, y] = qz[d, y * 2 + 1 - xh]
        plo[y, x, c * 2 + d] = qz[d, y * 2 + xh]

    def grp(xx, cc, d):
        return plo.at[:, xx, cc * 2 + d]

    def cb_send(d, n, xx):
        go(rc(grp(xx, c, d), grp(xx, c, d), cbs.at[d, n], cbr.at[d, n], dev_core))

    cb_groups = (x, xn, xp, xf)

    def xb_step(d):
        for dy in YS:
            yy = yo(dy)
            rc(qz.at[d, yy * 2 + 1 - xh], fd.at[d, yy], ybs.at[d, 1, yy], ybr.at[d, 1, yy], dev_y(yy)).wait_recv()
        go(rc(fd.at[d], grp(x, c, d), fbs.at[d], fbr.at[d], dev_xn))
        for dy in YS:
            yy = yo(dy)
            rc(qz.at[d, yy * 2 + xh], plo.at[yy, x, c * 2 + d], ybs.at[d, 0, yy], ybr.at[d, 0, yy], dev_y(yy)).wait_recv()
        go(rc(grp(x, c, d), grp(x, c, d), xbs.at[d, 0], xbr.at[d, 0], dev_xp))
        cb_send(d, 0, x)

    def xb2_step(d):
        rc(fd.at[d], grp(xn, c, d), fbs.at[d], fbr.at[d], dev_xn).wait_recv()
        go(rc(grp(xn, c, d), grp(xn, c, d), xbs.at[d, 1], xbr.at[d, 1], dev_xp))
        cb_send(d, 1, xn)

    def xb3_step(d):
        rc(grp(x, c, d), grp(xp, c, d), xbs.at[d, 0], xbr.at[d, 0], dev_xp).wait_recv()
        cb_send(d, 2, xp)
        rc(grp(xn, c, d), grp(xf, c, d), xbs.at[d, 1], xbr.at[d, 1], dev_xp).wait_recv()
        cb_send(d, 3, xf)

    couple(0)
    couple(1)
    yb_step(0)
    xb_step(0)
    yb_step(1)
    xb2_step(0)
    xb3_step(0)
    xb_step(1)
    xb2_step(1)
    xb3_step(1)
    for d in range(2):
        for n in range(4):
            rc(grp(cb_groups[n], oc, d), grp(cb_groups[n], oc, d), cbs.at[d, n], cbr.at[d, n], dev_core).wait_recv()

    def down(n, carry):
        cc = lax.div(n, 16)
        i = lax.rem(n, 16)
        lhs, rhs = [], []
        for j in range(4):
            e = list_s[cc, i * 4 + j]
            ey = lax.div(e, 16)
            ex = lax.rem(lax.div(e, 4), 4)
            ec = lax.rem(e, 4)
            lhs.append(plo[ey, ex, ec].reshape(128, 128))
            m = tr[cc, ey, ex, ec]
            rhs.append(jnp.concatenate([m[0], m[1]], axis=1))
        r = combine(
            jnp.dot(
                jnp.concatenate(lhs, axis=1), jnp.concatenate(rhs, axis=0), preferred_element_type=F32
            )
        )
        t = jnp.concatenate([r[:, 0].reshape(64, 128), r[:, 1].reshape(64, 128)], axis=0)
        out[cc, i] = t.T.astype(BF)
        return carry

    lax.fori_loop(0, 32, down, 0, unroll=4)
    for cp in pend:
        cp.wait_send()


def body(child_coef, transfer, child_dir, couple_src, couple_kind, couple_count, couple_table):
    flip = (2, 1, 0)
    src, kind = couple_src.transpose(flip), couple_kind.transpose(flip)
    tr = transfer.reshape(2, 4, 4, 4, 2, 128, 128)
    vm = pl.BlockSpec(memory_space=pltpu.VMEM)
    hbm = pl.BlockSpec(memory_space=pl.ANY)
    dma = pltpu.SemaphoreType.DMA

    def blk(*lead):
        return pltpu.VMEM(lead + (8, 16, 128), BF)

    return pl.pallas_call(
        kernel,
        out_shape=pltpu.VMEM((2, 16, 128, 128), BF),
        in_specs=[pl.BlockSpec(memory_space=pltpu.SMEM), vm, vm, vm, vm, hbm, hbm, hbm],
        out_specs=vm,
        scratch_shapes=[
            pltpu.VMEM((2, 16, 128, 128), BF),
            pltpu.VMEM((2, 8, 2, 128, 128), BF),
            pltpu.VMEM((2, 4, 4, 4, 2, 128, 128), BF),
            pltpu.VMEM((2, 16, 128, 128), BF),
            blk(2, 4, 2, 4),
            blk(2, 4, 4),
            blk(2, 2, 4),
            blk(2, 2, 4),
            blk(2, 4),
            blk(2, 4),
            blk(2, 4),
            blk(2, 8),
            pltpu.VMEM((2, 8, 8, 16, 128), BF),
            pltpu.VMEM((ZERO_SLOT + 1, 16, 128), F32),
            pltpu.VMEM((2, 8, 8, 16, 128), BF),
            blk(2, 8),
            blk(2, 4),
            blk(4, 4, 4),
            pltpu.VMEM((16, 128), jnp.int32),
            pltpu.VMEM((8, 16, 128), jnp.int32),
            pltpu.SMEM((8, 16, 128), jnp.int32),
            pltpu.VMEM((8, 128), jnp.int32),
            pltpu.SMEM((8, 128), jnp.int32),
            dma((6,)), dma((2,)),
            dma((2, 4)), dma((2, 4)),
            dma((2, 2)), dma((2, 2)),
            dma((2,)), dma((2,)),
            dma((2, 2, 4)), dma((2, 2, 4)),
            dma((2, 8)), dma((2, 8)),
            dma((8,)), dma((8,)),
            dma((2, 8)), dma((2, 8)),
            dma((2, 2, 4)), dma((2, 2, 4)),
            dma((2,)), dma((2,)),
            dma((2, 2)), dma((2, 2)),
            dma((2, 4)), dma((2, 4)),
        ],
        compiler_params=pltpu.CompilerParams(
            collective_id=0, has_side_effects=True, vmem_limit_bytes=56 * 1024 * 1024
        ),
        name="h2_pass",
    )(child_dir, child_dir, src, kind, couple_count.T, child_coef, couple_table, tr)


def solution(mesh):
    return jax.shard_map(
        body,
        mesh=mesh,
        in_specs=(
            P(("gx", "gy"), None, None, None),
            P(("gx", "gy"), None, None, None, None),
            P(("gx", "gy"), None),
            P("gx", "gy", None),
            P("gx", "gy", None),
            P("gx", "gy"),
            P("gy", None, None, None, None),
        ),
        out_specs=P(("gx", "gy"), None, None, None),
        check_vma=False,
    )
```

```python
import jax
import jax.numpy as jnp
from jax import lax
from jax.experimental import pallas as pl
from jax.experimental.pallas import tpu as pltpu
from jax.sharding import PartitionSpec as P

MESH = pl.DeviceIdType.MESH
NT = (((1,), (1,)), ((), ()))
BF = jnp.bfloat16
F32 = jnp.float32
ZERO_SLOT = 512


def combine(z):
    z = z.reshape(z.shape[0] // 16, 2, 8, 256)
    re, im = z[:, 0], z[:, 1]
    out_re = re[:, :, :128] - im[:, :, 128:]
    out_im = im[:, :, :128] + re[:, :, 128:]
    return jnp.concatenate([out_re[:, None], out_im[:, None]], axis=1)


def kernel(
    dir_s, dir_v, src_v, kind_v, count_v, coef_hbm, table_hbm, tr_hbm,
    out,
    coef, table, tr, vc, send_own, recv_c, tx, recv_x, fw, ry_m, ry_o, rz, pz, zk, lo, qz, fd, plo,
    idx_v, idx_all, idx_s, list_v, list_s,
    sem_ld, sem_sm,
    cs, cr, xs, xr, fs, fr, ys, yr, zs, zr, is_, ir,
    zbs, zbr, ybs, ybr, fbs, fbr, xbs, xbr, cbs, cbr,
):
    z = lax.axis_index("gx")
    g = lax.axis_index("gy")
    c = lax.rem(g, 2)
    x = lax.rem(lax.div(g, 2), 4)
    y = lax.div(g, 8)
    xp = x + 1 - 2 * lax.rem(x, 2)
    xn = 3 - x
    xf = 3 - xp
    xh = lax.div(x, 2)
    oc = 1 - c

    def gid(yy, xx, cc):
        return (yy * 4 + xx) * 2 + cc

    dev_core = (z, gid(y, x, oc))
    dev_xp = (z, gid(y, xp, c))
    dev_xn = (z, gid(y, xn, c))

    def yo(dy):
        return lax.rem(y + dy, 4)

    def zo(dz):
        return lax.rem(z + dz, 8)

    def dev_y(yy):
        return (z, gid(yy, x, c))

    def dev_z(zz):
        return (zz, g)

    def rc(src, dst, ss, rs, dev):
        return pltpu.make_async_remote_copy(
            src_ref=src, dst_ref=dst, send_sem=ss, recv_sem=rs, device_id=dev, device_id_type=MESH
        )

    pend = []

    def go(cp):
        cp.start()
        pend.append(cp)

    YS = (2, 1, 3)
    ZE = (4, 2, 6)
    ZO = (3, 5, 1, 7)
    ZR = (ZE, ZO)
    ZS = ZE + ZO
    pri = (xf, xp, xn, x)

    def slot(h):
        return lax.rem(z + h, 2)

    barrier = pltpu.get_barrier_semaphore()
    partners = [dev_core, dev_xp, dev_xn] + [dev_y(yo(dy)) for dy in YS] + [dev_z(zo(dz)) for dz in ZS]
    for dev in partners:
        pl.semaphore_signal(barrier, inc=1, device_id=dev, device_id_type=MESH)

    cp_coef = pltpu.make_async_copy(coef_hbm, coef, sem_ld.at[4])
    cp_coef.start()
    loads = []
    for k in range(4):
        cp = pltpu.make_async_copy(tr_hbm.at[:, :, pri[k]], tr.at[:, :, pri[k]], sem_ld.at[k])
        cp.start()
        loads.append(cp)

    cp_table = pltpu.make_async_copy(table_hbm, table, sem_ld.at[5])
    cp_table.start()

    for m in range(7):
        idx_v[2 * m : 2 * m + 2, 0:8] = jnp.where(
            count_v[...] > m, kind_v[m] * 64 + src_v[m], ZERO_SLOT
        )
    cp_coef.wait()

    def prep(n, carry):
        cc = lax.div(n, 16)
        i = lax.rem(n, 16)
        vt = coef[cc, i].astype(F32).T.reshape(2, 8, 8, 128)
        v = jnp.concatenate([vt[0][:, None], vt[1][:, None]], axis=1)
        vc[cc, i] = v.reshape(128, 128).astype(BF)
        return carry

    lax.fori_loop(0, 32, prep, 0, unroll=4)

    def up(d, k):
        def one(n, carry):
            yy = lax.rem(n, 4)
            first = lax.div(n, 4)
            cc = lax.rem(oc + first, 2)
            cd = cc * 2 + d
            e = yy * 16 + pri[k] * 4 + cd
            lhs = jnp.concatenate([vc[0, dir_s[0, e]], vc[1, dir_s[1, e]]], axis=1)
            rhs = jnp.concatenate(
                [tr[0, yy, pri[k], cd].reshape(256, 128), tr[1, yy, pri[k], cd].reshape(256, 128)], axis=1
            )
            r = combine(lax.dot_general(lhs, rhs, NT, preferred_element_type=F32))
            r = r.reshape(8, 16, 128).astype(BF)
            for h in range(2):
                send_own[d, slot(h), k, first, yy] = r[4 * h : 4 * h + 4]
            return carry

        lax.fori_loop(0, 8, one, 0, unroll=8)

    def core_copy(d, k):
        return rc(send_own.at[d, :, k, 0], recv_c.at[d, :, k], cs.at[d, k], cr.at[d, k], dev_core)

    def x_copy(d, r, k):
        return rc(tx.at[d, r, k], recv_x.at[d, r, k], xs.at[d, r, k], xr.at[d, r, k], dev_xp)

    def fw_copy(d, r):
        return rc(fw.at[d, r], ry_o.at[d, r], fs.at[d, r], fr.at[d, r], dev_xn)

    def t_step(d, k):
        core_copy(d, k).wait_recv()
        for r in range(2):
            tx[d, r, k] = (send_own[d, r, k, 1].astype(F32) + recv_c[d, r, k].astype(F32)).astype(BF)
            go(x_copy(d, r, k))

    def add3(d, r, k):
        return (
            send_own[d, r, k + 2, 1].astype(F32)
            + recv_c[d, r, k + 2].astype(F32)
            + recv_x[d, r, k].astype(F32)
        ).astype(BF)

    def f_step(d, r):
        if r == 0:
            core_copy(d, 2).wait_recv()
        x_copy(d, r, 0).wait_recv()
        fw[d, r] = add3(d, r, 0)
        go(fw_copy(d, r))

    def y_copy(d, r, kind, src, yy, arrive):
        p = (yy if arrive else y) * 2 + (xh if kind == 0 else 1 - xh)
        return rc(
            src.at[d, r, yy], rz.at[d, r, p],
            ys.at[d, r, kind, yy], yr.at[d, r, kind, yy if arrive else y], dev_y(yy),
        )

    def g_step(d, r):
        if r == 0:
            core_copy(d, 3).wait_recv()
        x_copy(d, r, 1).wait_recv()
        ry_m[d, r] = add3(d, r, 1)
        for dy in YS:
            go(y_copy(d, r, 0, ry_m, yo(dy), False))
        rz[d, r, y * 2 + xh] = ry_m[d, r, y]

    def h_step(d, r):
        fw_copy(d, r).wait_recv()
        for dy in YS:
            go(y_copy(d, r, 1, ry_o, yo(dy), False))
        rz[d, r, y * 2 + 1 - xh] = ry_o[d, r, y]

    def z_copy(d, dz, arrive):
        zz = zo(dz)
        zf = zz if arrive else z
        return rc(
            rz.at[d, dz % 2, :, lax.div(zz, 2)], pz.at[d, zf], zs.at[d, zz], zr.at[d, zf], dev_z(zz)
        )

    def z_send(d, r):
        for kind in range(2):
            for dy in YS:
                y_copy(d, r, kind, ry_m, yo(dy), True).wait_recv()
        for dz in ZR[r]:
            go(z_copy(d, dz, False))
        if r == 0:
            pz[d, z] = rz[d, 0, :, lax.div(z, 2)]

    def idx_copy(dz, arrive):
        zz = zo(dz)
        zf = zz if arrive else z
        return rc(idx_v, idx_all.at[zf], is_.at[zz], ir.at[zf], dev_z(zz))

    loads[0].wait()
    up(0, 0)
    pl.semaphore_wait(barrier, len(partners))
    go(core_copy(0, 0))
    loads[1].wait()
    up(0, 1)
    go(core_copy(0, 1))
    t_step(0, 0)
    loads[2].wait()
    up(0, 2)
    go(core_copy(0, 2))
    t_step(0, 1)
    for dz in ZS:
        go(idx_copy(dz, False))
    idx_all[z] = idx_v[...]
    loads[3].wait()
    up(0, 3)
    go(core_copy(0, 3))
    up(1, 0)
    go(core_copy(1, 0))
    f_step(0, 0)
    up(1, 1)
    go(core_copy(1, 1))
    f_step(0, 1)
    t_step(1, 0)
    up(1, 2)
    go(core_copy(1, 2))
    t_step(1, 1)
    g_step(0, 0)
    h_step(0, 0)
    up(1, 3)
    go(core_copy(1, 3))
    g_step(0, 1)
    h_step(0, 1)
    f_step(1, 0)

    lane = lax.broadcasted_iota(jnp.int32, (128, 128), 1)
    sub = lax.broadcasted_iota(jnp.int32, (128, 128), 0)
    for cc in range(2):
        list_v[cc : cc + 1, 0:64] = dir_v[cc : cc + 1, :]
        row = jnp.where(lane < 64, jnp.broadcast_to(list_v[cc : cc + 1, :], (128, 128)), 64)
        same = jnp.where((row == row.T) & (sub < lane), 1, 0)
        key = row * 4 + jnp.broadcast_to(jnp.sum(same, axis=0, keepdims=True), (128, 128))
        list_v[cc : cc + 1, :] = jnp.sum(jnp.where(key.T == lane, sub, 0), axis=0, keepdims=True)
    zk[ZERO_SLOT] = jnp.zeros((16, 128), F32)

    z_send(0, 0)
    f_step(1, 1)
    cp_list = pltpu.make_async_copy(list_v, list_s, sem_sm.at[0])
    cp_list.start()
    z_send(0, 1)
    g_step(1, 0)
    h_step(1, 0)
    g_step(1, 1)
    h_step(1, 1)
    cp_list.wait()
    for dz in ZS:
        idx_copy(dz, True).wait_recv()
    cp_idx = pltpu.make_async_copy(idx_all, idx_s, sem_sm.at[1])
    cp_idx.start()
    z_send(1, 0)
    cp_idx.wait()
    cp_table.wait()
    z_send(1, 1)

    def zb_copy(d, dz, arrive):
        zz = zo(dz)
        zf = zz if arrive else z
        return rc(
            lo.at[d, zz], qz.at[d, dz % 2, :, lax.div(zf, 2)], zbs.at[d, zz], zbr.at[d, zf], dev_z(zz)
        )

    def couple(d):
        for dz in ZS:
            z_copy(d, dz, True).wait_recv()

        def dense(k, carry):
            rhs = table[d, k].reshape(256, 128)
            for q in range(4):
                lhs = pz[d, q * 2 : q * 2 + 2].reshape(256, 128)
                r = combine(lax.dot_general(lhs, rhs, NT, preferred_element_type=F32))
                zk[pl.ds(k * 64 + q * 16, 16)] = r.reshape(16, 16, 128)
            return carry

        lax.fori_loop(0, 8, dense, 0, unroll=2)
        for dz in ZE + (0,) + ZO:
            zz = zo(dz)

            def row_sum(p, carry):
                acc = zk[idx_s[zz, d, p]]
                for m in range(1, 7):
                    acc = acc + zk[idx_s[zz, 2 * m + d, p]]
                lo[d, zz, p] = acc.astype(BF)
                return carry

            lax.fori_loop(0, 8, row_sum, 0, unroll=4)
            if dz:
                go(zb_copy(d, dz, False))
        qz[d, 0, :, lax.div(z, 2)] = lo[d, z]

    def yb_copy(d, r, kind, yy, arrive):
        yf = yy if arrive else y
        p = yy * 2 + (xh if kind == 0 else 1 - xh)
        dst = plo.at[r, yf, x, c * 2 + d] if kind == 0 else fd.at[d, r, yf]
        return rc(qz.at[d, r, p], dst, ybs.at[d, r, kind, yy], ybr.at[d, r, kind, yf], dev_y(yy))

    def yb_step(d, r):
        for dz in ZR[r]:
            zb_copy(d, dz, True).wait_recv()
        for kind in (1, 0):
            for dy in YS:
                go(yb_copy(d, r, kind, yo(dy), False))
        fd[d, r, y] = qz[d, r, y * 2 + 1 - xh]
        plo[r, y, x, c * 2 + d] = qz[d, r, y * 2 + xh]

    def grp(r, xx, cc, d):
        return plo.at[r, :, xx, cc * 2 + d]

    cb_groups = (x, xn, xp, xf)

    def cb_copy(d, r, n, cc):
        ref = grp(r, cb_groups[n], cc, d)
        return rc(ref, ref, cbs.at[d, r, n], cbr.at[d, r, n], dev_core)

    def fb_copy(d, r, xx):
        return rc(fd.at[d, r], grp(r, xx, c, d), fbs.at[d, r], fbr.at[d, r], dev_xn)

    def xb_copy(d, r, n, src, dst):
        return rc(grp(r, src, c, d), grp(r, dst, c, d), xbs.at[d, r, n], xbr.at[d, r, n], dev_xp)

    def xb_step(d, r):
        for dy in YS:
            yb_copy(d, r, 1, yo(dy), True).wait_recv()
        go(fb_copy(d, r, x))
        for dy in YS:
            yb_copy(d, r, 0, yo(dy), True).wait_recv()
        go(xb_copy(d, r, 0, x, x))
        go(cb_copy(d, r, 0, c))

    def xb2_step(d, r):
        fb_copy(d, r, xn).wait_recv()
        go(xb_copy(d, r, 1, xn, xn))
        go(cb_copy(d, r, 1, c))

    def xb3_step(d, r):
        xb_copy(d, r, 0, x, xp).wait_recv()
        go(cb_copy(d, r, 2, c))
        xb_copy(d, r, 1, xn, xf).wait_recv()
        go(cb_copy(d, r, 3, c))

    couple(0)
    couple(1)
    yb_step(0, 0)
    yb_step(0, 1)
    xb_step(0, 0)
    yb_step(1, 0)
    xb_step(0, 1)
    xb2_step(0, 0)
    yb_step(1, 1)
    xb_step(1, 0)
    xb2_step(0, 1)
    xb3_step(0, 0)
    xb_step(1, 1)
    xb2_step(1, 0)
    xb3_step(0, 1)
    xb2_step(1, 1)
    xb3_step(1, 0)
    xb3_step(1, 1)
    for d in range(2):
        for r in range(2):
            for n in range(4):
                cb_copy(d, r, n, oc).wait_recv()

    def down(n, carry):
        cc = lax.div(n, 16)
        i = lax.rem(n, 16)
        lhs, rhs = [], []
        for j in range(4):
            e = list_s[cc, i * 4 + j]
            ey = lax.div(e, 16)
            ex = lax.rem(lax.div(e, 4), 4)
            ec = lax.rem(e, 4)
            halves = [plo[slot(h), ey, ex, ec].reshape(64, 128) for h in range(2)]
            lhs.append(jnp.concatenate(halves, axis=0))
            m = tr[cc, ey, ex, ec]
            rhs.append(jnp.concatenate([m[0], m[1]], axis=1))
        r = combine(
            jnp.dot(
                jnp.concatenate(lhs, axis=1), jnp.concatenate(rhs, axis=0), preferred_element_type=F32
            )
        )
        t = jnp.concatenate([r[:, 0].reshape(64, 128), r[:, 1].reshape(64, 128)], axis=0)
        out[cc, i] = t.T.astype(BF)
        return carry

    lax.fori_loop(0, 32, down, 0, unroll=4)
    for cp in pend:
        cp.wait_send()


def body(child_coef, transfer, child_dir, couple_src, couple_kind, couple_count, couple_table):
    flip = (2, 1, 0)
    src, kind = couple_src.transpose(flip), couple_kind.transpose(flip)
    tr = transfer.reshape(2, 4, 4, 4, 2, 128, 128)
    vm = pl.BlockSpec(memory_space=pltpu.VMEM)
    hbm = pl.BlockSpec(memory_space=pl.ANY)
    dma = pltpu.SemaphoreType.DMA

    def blk(*lead):
        return pltpu.VMEM(lead + (4, 16, 128), BF)

    return pl.pallas_call(
        kernel,
        out_shape=pltpu.VMEM((2, 16, 128, 128), BF),
        in_specs=[pl.BlockSpec(memory_space=pltpu.SMEM), vm, vm, vm, vm, hbm, hbm, hbm],
        out_specs=vm,
        scratch_shapes=[
            pltpu.VMEM((2, 16, 128, 128), BF),
            pltpu.VMEM((2, 8, 2, 128, 128), BF),
            pltpu.VMEM((2, 4, 4, 4, 2, 128, 128), BF),
            pltpu.VMEM((2, 16, 128, 128), BF),
            blk(2, 2, 4, 2, 4),
            blk(2, 2, 4, 4),
            blk(2, 2, 2, 4),
            blk(2, 2, 2, 4),
            blk(2, 2, 4),
            blk(2, 2, 4),
            blk(2, 2, 4),
            blk(2, 2, 8),
            pltpu.VMEM((2, 8, 8, 16, 128), BF),
            pltpu.VMEM((ZERO_SLOT + 1, 16, 128), F32),
            pltpu.VMEM((2, 8, 8, 16, 128), BF),
            blk(2, 2, 8),
            blk(2, 2, 4),
            blk(2, 4, 4, 4),
            pltpu.VMEM((16, 128), jnp.int32),
            pltpu.VMEM((8, 16, 128), jnp.int32),
            pltpu.SMEM((8, 16, 128), jnp.int32),
            pltpu.VMEM((8, 128), jnp.int32),
            pltpu.SMEM((8, 128), jnp.int32),
            dma((6,)), dma((2,)),
            dma((2, 4)), dma((2, 4)),
            dma((2, 2, 2)), dma((2, 2, 2)),
            dma((2, 2)), dma((2, 2)),
            dma((2, 2, 2, 4)), dma((2, 2, 2, 4)),
            dma((2, 8)), dma((2, 8)),
            dma((8,)), dma((8,)),
            dma((2, 8)), dma((2, 8)),
            dma((2, 2, 2, 4)), dma((2, 2, 2, 4)),
            dma((2, 2)), dma((2, 2)),
            dma((2, 2, 2)), dma((2, 2, 2)),
            dma((2, 2, 4)), dma((2, 2, 4)),
        ],
        compiler_params=pltpu.CompilerParams(
            collective_id=0, has_side_effects=True, vmem_limit_bytes=56 * 1024 * 1024
        ),
        name="h2_pass",
    )(child_dir, child_dir, src, kind, couple_count.T, child_coef, couple_table, tr)


def solution(mesh):
    return jax.shard_map(
        body,
        mesh=mesh,
        in_specs=(
            P(("gx", "gy"), None, None, None),
            P(("gx", "gy"), None, None, None, None),
            P(("gx", "gy"), None),
            P("gx", "gy", None),
            P("gx", "gy", None),
            P("gx", "gy"),
            P("gy", None, None, None, None),
        ),
        out_specs=P(("gx", "gy"), None, None, None),
        check_vma=False,
    )
```

```python
import jax
import jax.numpy as jnp
from jax import lax
from jax.experimental import pallas as pl
from jax.experimental.pallas import tpu as pltpu
from jax.sharding import PartitionSpec as P

MESH = pl.DeviceIdType.MESH
NT = (((1,), (1,)), ((), ()))
BF = jnp.bfloat16
F32 = jnp.float32
ZERO_SLOT = 512


def combine(z):
    z = z.reshape(z.shape[0] // 16, 2, 8, 256)
    re, im = z[:, 0], z[:, 1]
    out_re = re[:, :, :128] - im[:, :, 128:]
    out_im = im[:, :, :128] + re[:, :, 128:]
    return jnp.concatenate([out_re[:, None], out_im[:, None]], axis=1)


def kernel(
    dir_s, dir_v, src_v, kind_v, count_v, coef_hbm, table_hbm, tr_hbm,
    out,
    coef, table, tr, vc, send_own, recv_c, tx, recv_x, fw, ry_m, rz, pz, zk, lo, qz, plo,
    idx_v, idx_all, idx_s, list_v, list_s,
    sem_ld, sem_sm,
    cs, cr, xs, xr, ys, yr, zs, zr, is_, ir,
    zbs, zbr, ybs, ybr, cbs, cbr,
):
    z = lax.axis_index("gx")
    g = lax.axis_index("gy")
    c = lax.rem(g, 2)
    x = lax.rem(lax.div(g, 2), 4)
    y = lax.div(g, 8)
    xp = x + 1 - 2 * lax.rem(x, 2)
    xn = 3 - x
    xf = 3 - xp
    xh = lax.div(x, 2)
    oc = 1 - c

    def gid(yy, xx, cc):
        return (yy * 4 + xx) * 2 + cc

    dev_core = (z, gid(y, x, oc))
    dev_xp = (z, gid(y, xp, c))

    def yo(dy):
        return lax.rem(y + dy, 4)

    def zo(dz):
        return lax.rem(z + dz, 8)

    rel = (x, xp, xn, xf)

    def dev_n(n, dy):
        return (z, gid(yo(dy), rel[n], c))

    def dev_z(zz):
        return (zz, g)

    def rc(src, dst, ss, rs, dev):
        return pltpu.make_async_remote_copy(
            src_ref=src, dst_ref=dst, send_sem=ss, recv_sem=rs, device_id=dev, device_id_type=MESH
        )

    pend = []

    def go(cp):
        cp.start()
        pend.append(cp)

    YS = (2, 1, 3)
    ZE = (4, 2, 6)
    ZO = (3, 5, 1, 7)
    ZR = (ZE, ZO)
    ZS = ZE + ZO
    pri = (xf, xp, xn, x)

    def slot(h):
        return lax.rem(z + h, 2)

    barrier = pltpu.get_barrier_semaphore()
    partners = [dev_core] + [dev_z(zo(dz)) for dz in ZS]
    partners += [dev_n(n, dy) for n in range(4) for dy in range(4) if n or dy]
    for dev in partners:
        pl.semaphore_signal(barrier, inc=1, device_id=dev, device_id_type=MESH)

    cp_coef = pltpu.make_async_copy(coef_hbm, coef, sem_ld.at[4])
    cp_coef.start()
    loads = []
    for k in range(4):
        cp = pltpu.make_async_copy(tr_hbm.at[:, :, pri[k]], tr.at[:, :, pri[k]], sem_ld.at[k])
        cp.start()
        loads.append(cp)

    cp_table = pltpu.make_async_copy(table_hbm, table, sem_ld.at[5])
    cp_table.start()

    for m in range(7):
        idx_v[2 * m : 2 * m + 2, 0:8] = jnp.where(
            count_v[...] > m, kind_v[m] * 64 + src_v[m], ZERO_SLOT
        )
    cp_coef.wait()

    def prep(n, carry):
        cc = lax.div(n, 16)
        i = lax.rem(n, 16)
        vt = coef[cc, i].astype(F32).T.reshape(2, 8, 8, 128)
        v = jnp.concatenate([vt[0][:, None], vt[1][:, None]], axis=1)
        vc[cc, i] = v.reshape(128, 128).astype(BF)
        return carry

    lax.fori_loop(0, 32, prep, 0, unroll=4)

    def up(d, k):
        def one(n, carry):
            yy = lax.rem(n, 4)
            first = lax.div(n, 4)
            cc = lax.rem(oc + first, 2)
            cd = cc * 2 + d
            e = yy * 16 + pri[k] * 4 + cd
            lhs = jnp.concatenate([vc[0, dir_s[0, e]], vc[1, dir_s[1, e]]], axis=1)
            rhs = jnp.concatenate(
                [tr[0, yy, pri[k], cd].reshape(256, 128), tr[1, yy, pri[k], cd].reshape(256, 128)], axis=1
            )
            r = combine(lax.dot_general(lhs, rhs, NT, preferred_element_type=F32))
            r = r.reshape(8, 16, 128).astype(BF)
            for h in range(2):
                send_own[d, slot(h), k, first, yy] = r[4 * h : 4 * h + 4]
            return carry

        lax.fori_loop(0, 8, one, 0, unroll=8)

    def core_copy(d, k):
        return rc(send_own.at[d, :, k, 0], recv_c.at[d, :, k], cs.at[d, k], cr.at[d, k], dev_core)

    def x_copy(d, r, k):
        return rc(tx.at[d, r, k], recv_x.at[d, r, k], xs.at[d, r, k], xr.at[d, r, k], dev_xp)

    def t_step(d, k):
        core_copy(d, k).wait_recv()
        for r in range(2):
            tx[d, r, k] = (send_own[d, r, k, 1].astype(F32) + recv_c[d, r, k].astype(F32)).astype(BF)
            go(x_copy(d, r, k))

    def add3(d, r, k):
        return (
            send_own[d, r, k + 2, 1].astype(F32)
            + recv_c[d, r, k + 2].astype(F32)
            + recv_x[d, r, k].astype(F32)
        ).astype(BF)

    def y_copy(d, r, n, dy, arrive):
        yy = yo(dy)
        yf = yy if arrive else y
        src = fw if n else ry_m
        p = yf * 2 + (1 - xh if n and arrive else xh)
        return rc(
            src.at[d, r, yy], rz.at[d, r, p], ys.at[d, r, n // 2, yy], yr.at[d, r, n // 2, yf], dev_n(n, dy)
        )

    def f_step(d, r):
        if r == 0:
            core_copy(d, 2).wait_recv()
        x_copy(d, r, 0).wait_recv()
        fw[d, r] = add3(d, r, 0)
        for dy in YS + (0,):
            go(y_copy(d, r, 2, dy, False))

    def g_step(d, r):
        if r == 0:
            core_copy(d, 3).wait_recv()
        x_copy(d, r, 1).wait_recv()
        ry_m[d, r] = add3(d, r, 1)
        for dy in YS:
            go(y_copy(d, r, 0, dy, False))
        rz[d, r, y * 2 + xh] = ry_m[d, r, y]

    def z_copy(d, dz, arrive):
        zz = zo(dz)
        zf = zz if arrive else z
        return rc(
            rz.at[d, dz % 2, :, lax.div(zz, 2)], pz.at[d, zf], zs.at[d, zz], zr.at[d, zf], dev_z(zz)
        )

    def z_send(d, r):
        for dy in YS + (0,):
            y_copy(d, r, 2, dy, True).wait_recv()
        for dy in YS:
            y_copy(d, r, 0, dy, True).wait_recv()
        for dz in ZR[r]:
            go(z_copy(d, dz, False))
        if r == 0:
            pz[d, z] = rz[d, 0, :, lax.div(z, 2)]

    def idx_copy(dz, arrive):
        zz = zo(dz)
        zf = zz if arrive else z
        return rc(idx_v, idx_all.at[zf], is_.at[zz], ir.at[zf], dev_z(zz))

    loads[0].wait()
    up(0, 0)
    pl.semaphore_wait(barrier, len(partners))
    go(core_copy(0, 0))
    loads[1].wait()
    up(0, 1)
    go(core_copy(0, 1))
    t_step(0, 0)
    loads[2].wait()
    up(0, 2)
    go(core_copy(0, 2))
    t_step(0, 1)
    for dz in ZS:
        go(idx_copy(dz, False))
    idx_all[z] = idx_v[...]
    loads[3].wait()
    up(0, 3)
    go(core_copy(0, 3))
    up(1, 0)
    go(core_copy(1, 0))
    f_step(0, 0)
    up(1, 1)
    go(core_copy(1, 1))
    f_step(0, 1)
    t_step(1, 0)
    up(1, 2)
    go(core_copy(1, 2))
    t_step(1, 1)
    g_step(0, 0)
    up(1, 3)
    go(core_copy(1, 3))
    g_step(0, 1)
    f_step(1, 0)

    lane = lax.broadcasted_iota(jnp.int32, (128, 128), 1)
    sub = lax.broadcasted_iota(jnp.int32, (128, 128), 0)
    for cc in range(2):
        list_v[cc : cc + 1, 0:64] = dir_v[cc : cc + 1, :]
        row = jnp.where(lane < 64, jnp.broadcast_to(list_v[cc : cc + 1, :], (128, 128)), 64)
        same = jnp.where((row == row.T) & (sub < lane), 1, 0)
        key = row * 4 + jnp.broadcast_to(jnp.sum(same, axis=0, keepdims=True), (128, 128))
        list_v[cc : cc + 1, :] = jnp.sum(jnp.where(key.T == lane, sub, 0), axis=0, keepdims=True)
    zk[ZERO_SLOT] = jnp.zeros((16, 128), F32)

    z_send(0, 0)
    f_step(1, 1)
    cp_list = pltpu.make_async_copy(list_v, list_s, sem_sm.at[0])
    cp_list.start()
    z_send(0, 1)
    g_step(1, 0)
    g_step(1, 1)
    cp_list.wait()
    for dz in ZS:
        idx_copy(dz, True).wait_recv()
    cp_idx = pltpu.make_async_copy(idx_all, idx_s, sem_sm.at[1])
    cp_idx.start()
    z_send(1, 0)
    cp_idx.wait()
    cp_table.wait()
    z_send(1, 1)

    def zb_copy(d, dz, arrive):
        zz = zo(dz)
        zf = zz if arrive else z
        return rc(
            lo.at[d, zz], qz.at[d, dz % 2, :, lax.div(zf, 2)], zbs.at[d, zz], zbr.at[d, zf], dev_z(zz)
        )

    def couple(d):
        for dz in ZS:
            z_copy(d, dz, True).wait_recv()

        def dense(k, carry):
            rhs = table[d, k].reshape(256, 128)
            for q in range(4):
                lhs = pz[d, q * 2 : q * 2 + 2].reshape(256, 128)
                r = combine(lax.dot_general(lhs, rhs, NT, preferred_element_type=F32))
                zk[pl.ds(k * 64 + q * 16, 16)] = r.reshape(16, 16, 128)
            return carry

        lax.fori_loop(0, 8, dense, 0, unroll=2)
        for dz in ZE + (0,) + ZO:
            zz = zo(dz)

            def row_sum(p, carry):
                acc = zk[idx_s[zz, d, p]]
                for m in range(1, 7):
                    acc = acc + zk[idx_s[zz, 2 * m + d, p]]
                lo[d, zz, p] = acc.astype(BF)
                return carry

            lax.fori_loop(0, 8, row_sum, 0, unroll=4)
            if dz:
                go(zb_copy(d, dz, False))
        qz[d, 0, :, lax.div(z, 2)] = lo[d, z]

    NS = (3, 2, 1, 0)

    def yb_copy(d, r, n, dy, arrive):
        yy = yo(dy)
        yf, xs_ = (yy, rel[n]) if arrive else (y, x)
        p = yy * 2 + (xh if n < 2 else 1 - xh)
        return rc(
            qz.at[d, r, p], plo.at[r, yf, xs_, c * 2 + d],
            ybs.at[d, r, n, yy], ybr.at[d, r, n, yf], dev_n(n, dy),
        )

    def yb_step(d, r):
        for dz in ZR[r]:
            zb_copy(d, dz, True).wait_recv()
        for n in NS:
            for dy in YS + (0,):
                if n or dy:
                    go(yb_copy(d, r, n, dy, False))
        plo[r, y, x, c * 2 + d] = qz[d, r, y * 2 + xh]

    def grp(r, xx, cc, d):
        return plo.at[r, :, xx, cc * 2 + d]


    def cb_copy(d, r, n, cc):
        ref = grp(r, rel[n], cc, d)
        return rc(ref, ref, cbs.at[d, r, n], cbr.at[d, r, n], dev_core)

    def xb_step(d, r):
        for n in NS:
            for dy in YS + (0,):
                if n or dy:
                    yb_copy(d, r, n, dy, True).wait_recv()
            go(cb_copy(d, r, n, c))

    couple(0)
    couple(1)
    yb_step(0, 0)
    yb_step(0, 1)
    xb_step(0, 0)
    yb_step(1, 0)
    xb_step(0, 1)
    yb_step(1, 1)
    xb_step(1, 0)
    xb_step(1, 1)
    for d in range(2):
        for r in range(2):
            for n in range(4):
                cb_copy(d, r, n, oc).wait_recv()

    def down(n, carry):
        cc = lax.div(n, 16)
        i = lax.rem(n, 16)
        lhs, rhs = [], []
        for j in range(4):
            e = list_s[cc, i * 4 + j]
            ey = lax.div(e, 16)
            ex = lax.rem(lax.div(e, 4), 4)
            ec = lax.rem(e, 4)
            halves = [plo[slot(h), ey, ex, ec].reshape(64, 128) for h in range(2)]
            lhs.append(jnp.concatenate(halves, axis=0))
            m = tr[cc, ey, ex, ec]
            rhs.append(jnp.concatenate([m[0], m[1]], axis=1))
        r = combine(
            jnp.dot(
                jnp.concatenate(lhs, axis=1), jnp.concatenate(rhs, axis=0), preferred_element_type=F32
            )
        )
        t = jnp.concatenate([r[:, 0].reshape(64, 128), r[:, 1].reshape(64, 128)], axis=0)
        out[cc, i] = t.T.astype(BF)
        return carry

    lax.fori_loop(0, 32, down, 0, unroll=4)
    for cp in pend:
        cp.wait_send()


def body(child_coef, transfer, child_dir, couple_src, couple_kind, couple_count, couple_table):
    flip = (2, 1, 0)
    src, kind = couple_src.transpose(flip), couple_kind.transpose(flip)
    tr = transfer.reshape(2, 4, 4, 4, 2, 128, 128)
    vm = pl.BlockSpec(memory_space=pltpu.VMEM)
    hbm = pl.BlockSpec(memory_space=pl.ANY)
    dma = pltpu.SemaphoreType.DMA

    def blk(*lead):
        return pltpu.VMEM(lead + (4, 16, 128), BF)

    return pl.pallas_call(
        kernel,
        out_shape=pltpu.VMEM((2, 16, 128, 128), BF),
        in_specs=[pl.BlockSpec(memory_space=pltpu.SMEM), vm, vm, vm, vm, hbm, hbm, hbm],
        out_specs=vm,
        scratch_shapes=[
            pltpu.VMEM((2, 16, 128, 128), BF),
            pltpu.VMEM((2, 8, 2, 128, 128), BF),
            pltpu.VMEM((2, 4, 4, 4, 2, 128, 128), BF),
            pltpu.VMEM((2, 16, 128, 128), BF),
            blk(2, 2, 4, 2, 4),
            blk(2, 2, 4, 4),
            blk(2, 2, 2, 4),
            blk(2, 2, 2, 4),
            blk(2, 2, 4),
            blk(2, 2, 4),
            blk(2, 2, 8),
            pltpu.VMEM((2, 8, 8, 16, 128), BF),
            pltpu.VMEM((ZERO_SLOT + 1, 16, 128), F32),
            pltpu.VMEM((2, 8, 8, 16, 128), BF),
            blk(2, 2, 8),
            blk(2, 4, 4, 4),
            pltpu.VMEM((16, 128), jnp.int32),
            pltpu.VMEM((8, 16, 128), jnp.int32),
            pltpu.SMEM((8, 16, 128), jnp.int32),
            pltpu.VMEM((8, 128), jnp.int32),
            pltpu.SMEM((8, 128), jnp.int32),
            dma((6,)), dma((2,)),
            dma((2, 4)), dma((2, 4)),
            dma((2, 2, 2)), dma((2, 2, 2)),
            dma((2, 2, 2, 4)), dma((2, 2, 2, 4)),
            dma((2, 8)), dma((2, 8)),
            dma((8,)), dma((8,)),
            dma((2, 8)), dma((2, 8)),
            dma((2, 2, 4, 4)), dma((2, 2, 4, 4)),
            dma((2, 2, 4)), dma((2, 2, 4)),
        ],
        compiler_params=pltpu.CompilerParams(
            collective_id=0, has_side_effects=True, vmem_limit_bytes=56 * 1024 * 1024
        ),
        name="h2_pass",
    )(child_dir, child_dir, src, kind, couple_count.T, child_coef, couple_table, tr)


def solution(mesh):
    return jax.shard_map(
        body,
        mesh=mesh,
        in_specs=(
            P(("gx", "gy"), None, None, None),
            P(("gx", "gy"), None, None, None, None),
            P(("gx", "gy"), None),
            P("gx", "gy", None),
            P("gx", "gy", None),
            P("gx", "gy"),
            P("gy", None, None, None, None),
        ),
        out_specs=P(("gx", "gy"), None, None, None),
        check_vma=False,
    )
```

```python
import jax
import jax.numpy as jnp
from jax import lax
from jax.experimental import pallas as pl
from jax.experimental.pallas import tpu as pltpu
from jax.sharding import PartitionSpec as P

MESH = pl.DeviceIdType.MESH
NT = (((1,), (1,)), ((), ()))
BF = jnp.bfloat16
F32 = jnp.float32
ZERO_SLOT = 512


def combine(z):
    z = z.reshape(z.shape[0] // 16, 2, 8, 256)
    re, im = z[:, 0], z[:, 1]
    out_re = re[:, :, :128] - im[:, :, 128:]
    out_im = im[:, :, :128] + re[:, :, 128:]
    return jnp.concatenate([out_re[:, None], out_im[:, None]], axis=1)


def kernel(
    dir_s, dir_v, src_v, kind_v, count_v, coef_hbm, table_hbm, tr_hbm,
    out,
    coef, table, tr, vc, send_own, recv_c, tx, recv_x, fw, ry_m, rz, pz, zk, lo, qz, plo,
    idx_v, idx_all, idx_s, list_v, list_s,
    sem_ld, sem_sm,
    cs, cr, xs, xr, ys, yr, zs, zr, is_, ir,
    zbs, zbr, ybs, ybr, cbs, cbr,
):
    z = lax.axis_index("gx")
    g = lax.axis_index("gy")
    c = lax.rem(g, 2)
    x = lax.rem(lax.div(g, 2), 4)
    y = lax.div(g, 8)
    xp = x + 1 - 2 * lax.rem(x, 2)
    xn = 3 - x
    xf = 3 - xp
    xh = lax.div(x, 2)
    oc = 1 - c

    def gid(yy, xx, cc):
        return (yy * 4 + xx) * 2 + cc

    dev_core = (z, gid(y, x, oc))
    dev_xp = (z, gid(y, xp, c))

    def yo(dy):
        return lax.rem(y + dy, 4)

    def zo(dz):
        return lax.rem(z + dz, 8)

    rel = (x, xp, xn, xf)

    def dev_n(n, dy):
        return (z, gid(yo(dy), rel[n], c))

    def dev_z(zz):
        return (zz, g)

    def rc(src, dst, ss, rs, dev):
        return pltpu.make_async_remote_copy(
            src_ref=src, dst_ref=dst, send_sem=ss, recv_sem=rs, device_id=dev, device_id_type=MESH
        )

    pend = []

    def go(cp):
        cp.start()
        pend.append(cp)

    def drain():
        for cp in pend:
            cp.wait_send()
        pend.clear()

    YS = (2, 1, 3)
    ZE = (4, 2, 6)
    ZO = (3, 5, 1, 7)
    ZR = (ZE, ZO)
    ZS = ZE + ZO
    pri = (xf, xp, xn, x)

    def slot(h):
        return lax.rem(z + h, 2)

    barrier = pltpu.get_barrier_semaphore()
    partners = [dev_core] + [dev_z(zo(dz)) for dz in ZS]
    partners += [dev_n(n, dy) for n in range(4) for dy in range(4) if n or dy]
    for dev in partners:
        pl.semaphore_signal(barrier, inc=1, device_id=dev, device_id_type=MESH)

    cp_coef = pltpu.make_async_copy(coef_hbm, coef, sem_ld.at[4])
    cp_coef.start()
    loads = []
    for k in range(4):
        cp = pltpu.make_async_copy(tr_hbm.at[:, :, pri[k]], tr.at[:, :, pri[k]], sem_ld.at[k])
        cp.start()
        loads.append(cp)

    cp_table = pltpu.make_async_copy(table_hbm, table, sem_ld.at[5])
    cp_table.start()

    for m in range(7):
        idx_v[2 * m : 2 * m + 2, 0:8] = jnp.where(
            count_v[...] > m, kind_v[m] * 64 + src_v[m], ZERO_SLOT
        )
    cp_coef.wait()

    def prep(n, carry):
        cc = lax.div(n, 16)
        i = lax.rem(n, 16)
        vt = coef[cc, i].astype(F32).T.reshape(2, 8, 8, 128)
        v = jnp.concatenate([vt[0][:, None], vt[1][:, None]], axis=1)
        vc[cc, i] = v.reshape(128, 128).astype(BF)
        return carry

    lax.fori_loop(0, 32, prep, 0, unroll=4)

    def up(d, k):
        def one(n, carry):
            yy = lax.rem(n, 4)
            first = lax.div(n, 4)
            cc = lax.rem(oc + first, 2)
            cd = cc * 2 + d
            e = yy * 16 + pri[k] * 4 + cd
            lhs = jnp.concatenate([vc[0, dir_s[0, e]], vc[1, dir_s[1, e]]], axis=1)
            rhs = jnp.concatenate(
                [tr[0, yy, pri[k], cd].reshape(256, 128), tr[1, yy, pri[k], cd].reshape(256, 128)], axis=1
            )
            r = combine(lax.dot_general(lhs, rhs, NT, preferred_element_type=F32))
            r = r.reshape(8, 16, 128).astype(BF)
            for h in range(2):
                send_own[d, slot(h), k, first, yy] = r[4 * h : 4 * h + 4]
            return carry

        lax.fori_loop(0, 8, one, 0, unroll=8)

    def core_copy(d, k):
        return rc(send_own.at[d, :, k, 0], recv_c.at[d, :, k], cs.at[d, k], cr.at[d, k], dev_core)

    def x_copy(d, r, k):
        return rc(tx.at[d, r, k], recv_x.at[d, r, k], xs.at[d, r, k], xr.at[d, r, k], dev_xp)

    def t_step(d, k):
        core_copy(d, k).wait_recv()
        for r in range(2):
            tx[d, r, k] = (send_own[d, r, k, 1].astype(F32) + recv_c[d, r, k].astype(F32)).astype(BF)
            go(x_copy(d, r, k))

    def add3(d, r, k):
        return (
            send_own[d, r, k + 2, 1].astype(F32)
            + recv_c[d, r, k + 2].astype(F32)
            + recv_x[d, r, k].astype(F32)
        ).astype(BF)

    def y_copy(d, r, n, dy, arrive):
        yy = yo(dy)
        yf = yy if arrive else y
        src = fw if n else ry_m
        p = yf * 2 + (1 - xh if n and arrive else xh)
        return rc(
            src.at[d, r, yy], rz.at[d, r, p], ys.at[d, r, n // 2, yy], yr.at[d, r, n // 2, yf], dev_n(n, dy)
        )

    def f_step(d, r):
        if r == 0:
            core_copy(d, 2).wait_recv()
        x_copy(d, r, 0).wait_recv()
        fw[d, r] = add3(d, r, 0)
        for dy in YS + (0,):
            go(y_copy(d, r, 2, dy, False))

    def g_step(d, r):
        if r == 0:
            core_copy(d, 3).wait_recv()
        x_copy(d, r, 1).wait_recv()
        ry_m[d, r] = add3(d, r, 1)
        for dy in YS:
            go(y_copy(d, r, 0, dy, False))
        rz[d, r, y * 2 + xh] = ry_m[d, r, y]

    def z_copy(d, dz, arrive):
        zz = zo(dz)
        zf = zz if arrive else z
        return rc(
            rz.at[d, dz % 2, :, lax.div(zz, 2)], pz.at[d, zf], zs.at[d, zz], zr.at[d, zf], dev_z(zz)
        )

    def z_send(d, r):
        for dy in YS + (0,):
            y_copy(d, r, 2, dy, True).wait_recv()
        for dy in YS:
            y_copy(d, r, 0, dy, True).wait_recv()
        for dz in ZR[r]:
            go(z_copy(d, dz, False))
        if r == 0:
            pz[d, z] = rz[d, 0, :, lax.div(z, 2)]

    def idx_copy(dz, arrive):
        zz = zo(dz)
        zf = zz if arrive else z
        return rc(idx_v, idx_all.at[zf], is_.at[zz], ir.at[zf], dev_z(zz))

    loads[0].wait()
    up(0, 0)
    pl.semaphore_wait(barrier, len(partners))
    go(core_copy(0, 0))
    loads[1].wait()
    up(0, 1)
    go(core_copy(0, 1))
    t_step(0, 0)
    loads[2].wait()
    up(0, 2)
    go(core_copy(0, 2))
    t_step(0, 1)
    for dz in ZS:
        go(idx_copy(dz, False))
    idx_all[z] = idx_v[...]
    loads[3].wait()
    up(0, 3)
    go(core_copy(0, 3))
    up(1, 0)
    go(core_copy(1, 0))
    f_step(0, 0)
    up(1, 1)
    go(core_copy(1, 1))
    f_step(0, 1)
    t_step(1, 0)
    up(1, 2)
    go(core_copy(1, 2))
    t_step(1, 1)
    g_step(0, 0)
    up(1, 3)
    go(core_copy(1, 3))
    g_step(0, 1)
    f_step(1, 0)

    lane = lax.broadcasted_iota(jnp.int32, (128, 128), 1)
    sub = lax.broadcasted_iota(jnp.int32, (128, 128), 0)
    for cc in range(2):
        list_v[cc : cc + 1, 0:64] = dir_v[cc : cc + 1, :]
        row = jnp.where(lane < 64, jnp.broadcast_to(list_v[cc : cc + 1, :], (128, 128)), 64)
        same = jnp.where((row == row.T) & (sub < lane), 1, 0)
        key = row * 4 + jnp.broadcast_to(jnp.sum(same, axis=0, keepdims=True), (128, 128))
        list_v[cc : cc + 1, :] = jnp.sum(jnp.where(key.T == lane, sub, 0), axis=0, keepdims=True)
    zk[ZERO_SLOT] = jnp.zeros((16, 128), F32)

    z_send(0, 0)
    f_step(1, 1)
    cp_list = pltpu.make_async_copy(list_v, list_s, sem_sm.at[0])
    cp_list.start()
    z_send(0, 1)
    g_step(1, 0)
    g_step(1, 1)
    cp_list.wait()
    for dz in ZS:
        idx_copy(dz, True).wait_recv()
    cp_idx = pltpu.make_async_copy(idx_all, idx_s, sem_sm.at[1])
    cp_idx.start()
    z_send(1, 0)
    cp_idx.wait()
    cp_table.wait()
    z_send(1, 1)

    def zb_copy(d, dz, arrive):
        zz = zo(dz)
        zf = zz if arrive else z
        return rc(
            lo.at[d, zz], qz.at[d, dz % 2, :, lax.div(zf, 2)], zbs.at[d, zz], zbr.at[d, zf], dev_z(zz)
        )

    def couple(d):
        for dz in ZS:
            z_copy(d, dz, True).wait_recv()

        def dense(k, carry):
            rhs = table[d, k].reshape(256, 128)
            for q in range(4):
                lhs = pz[d, q * 2 : q * 2 + 2].reshape(256, 128)
                r = combine(lax.dot_general(lhs, rhs, NT, preferred_element_type=F32))
                zk[pl.ds(k * 64 + q * 16, 16)] = r.reshape(16, 16, 128)
            return carry

        lax.fori_loop(0, 8, dense, 0, unroll=2)
        for dz in ZE + (0,) + ZO:
            zz = zo(dz)

            def row_sum(p, carry):
                acc = zk[idx_s[zz, d, p]]
                for m in range(1, 7):
                    acc = acc + zk[idx_s[zz, 2 * m + d, p]]
                lo[d, zz, p] = acc.astype(BF)
                return carry

            lax.fori_loop(0, 8, row_sum, 0, unroll=4)
            if dz:
                go(zb_copy(d, dz, False))
        qz[d, 0, :, lax.div(z, 2)] = lo[d, z]

    NS = (3, 2, 1, 0)

    def yb_copy(d, r, n, dy, arrive):
        yy = yo(dy)
        yf, xs_ = (yy, rel[n]) if arrive else (y, x)
        p = yy * 2 + (xh if n < 2 else 1 - xh)
        return rc(
            qz.at[d, r, p], plo.at[r, yf, xs_, c * 2 + d],
            ybs.at[d, r, n, yy], ybr.at[d, r, n, yf], dev_n(n, dy),
        )

    def yb_step(d, r):
        for dz in ZR[r]:
            zb_copy(d, dz, True).wait_recv()
        for n in NS:
            for dy in YS + (0,):
                if n or dy:
                    go(yb_copy(d, r, n, dy, False))
        plo[r, y, x, c * 2 + d] = qz[d, r, y * 2 + xh]

    def grp(r, xx, cc, d):
        return plo.at[r, :, xx, cc * 2 + d]


    def cb_copy(d, r, n, cc):
        ref = grp(r, rel[n], cc, d)
        return rc(ref, ref, cbs.at[d, r, n], cbr.at[d, r, n], dev_core)

    def xb_step(d, r):
        for n in NS:
            for dy in YS + (0,):
                if n or dy:
                    yb_copy(d, r, n, dy, True).wait_recv()
            go(cb_copy(d, r, n, c))

    couple(0)
    couple(1)
    yb_step(0, 0)
    yb_step(0, 1)
    xb_step(0, 0)
    yb_step(1, 0)
    xb_step(0, 1)
    yb_step(1, 1)
    xb_step(1, 0)
    drain()
    xb_step(1, 1)
    for d in range(2):
        for r in range(2):
            for n in range(4):
                cb_copy(d, r, n, oc).wait_recv()

    drain()

    def down(n, carry):
        cc = lax.div(n, 16)
        i = lax.rem(n, 16)
        lhs, rhs = [], []
        for j in range(4):
            e = list_s[cc, i * 4 + j]
            ey = lax.div(e, 16)
            ex = lax.rem(lax.div(e, 4), 4)
            ec = lax.rem(e, 4)
            halves = [plo[slot(h), ey, ex, ec].reshape(64, 128) for h in range(2)]
            lhs.append(jnp.concatenate(halves, axis=0))
            m = tr[cc, ey, ex, ec]
            rhs.append(jnp.concatenate([m[0], m[1]], axis=1))
        r = combine(
            jnp.dot(
                jnp.concatenate(lhs, axis=1), jnp.concatenate(rhs, axis=0), preferred_element_type=F32
            )
        )
        t = jnp.concatenate([r[:, 0].reshape(64, 128), r[:, 1].reshape(64, 128)], axis=0)
        out[cc, i] = t.T.astype(BF)
        return carry

    lax.fori_loop(0, 32, down, 0, unroll=8)


def body(child_coef, transfer, child_dir, couple_src, couple_kind, couple_count, couple_table):
    flip = (2, 1, 0)
    src, kind = couple_src.transpose(flip), couple_kind.transpose(flip)
    tr = transfer.reshape(2, 4, 4, 4, 2, 128, 128)
    vm = pl.BlockSpec(memory_space=pltpu.VMEM)
    hbm = pl.BlockSpec(memory_space=pl.ANY)
    dma = pltpu.SemaphoreType.DMA

    def blk(*lead):
        return pltpu.VMEM(lead + (4, 16, 128), BF)

    return pl.pallas_call(
        kernel,
        out_shape=pltpu.VMEM((2, 16, 128, 128), BF),
        in_specs=[pl.BlockSpec(memory_space=pltpu.SMEM), vm, vm, vm, vm, hbm, hbm, hbm],
        out_specs=vm,
        scratch_shapes=[
            pltpu.VMEM((2, 16, 128, 128), BF),
            pltpu.VMEM((2, 8, 2, 128, 128), BF),
            pltpu.VMEM((2, 4, 4, 4, 2, 128, 128), BF),
            pltpu.VMEM((2, 16, 128, 128), BF),
            blk(2, 2, 4, 2, 4),
            blk(2, 2, 4, 4),
            blk(2, 2, 2, 4),
            blk(2, 2, 2, 4),
            blk(2, 2, 4),
            blk(2, 2, 4),
            blk(2, 2, 8),
            pltpu.VMEM((2, 8, 8, 16, 128), BF),
            pltpu.VMEM((ZERO_SLOT + 1, 16, 128), F32),
            pltpu.VMEM((2, 8, 8, 16, 128), BF),
            blk(2, 2, 8),
            blk(2, 4, 4, 4),
            pltpu.VMEM((16, 128), jnp.int32),
            pltpu.VMEM((8, 16, 128), jnp.int32),
            pltpu.SMEM((8, 16, 128), jnp.int32),
            pltpu.VMEM((8, 128), jnp.int32),
            pltpu.SMEM((8, 128), jnp.int32),
            dma((6,)), dma((2,)),
            dma((2, 4)), dma((2, 4)),
            dma((2, 2, 2)), dma((2, 2, 2)),
            dma((2, 2, 2, 4)), dma((2, 2, 2, 4)),
            dma((2, 8)), dma((2, 8)),
            dma((8,)), dma((8,)),
            dma((2, 8)), dma((2, 8)),
            dma((2, 2, 4, 4)), dma((2, 2, 4, 4)),
            dma((2, 2, 4)), dma((2, 2, 4)),
        ],
        compiler_params=pltpu.CompilerParams(
            collective_id=0, has_side_effects=True, vmem_limit_bytes=56 * 1024 * 1024
        ),
        name="h2_pass",
    )(child_dir, child_dir, src, kind, couple_count.T, child_coef, couple_table, tr)


def solution(mesh):
    return jax.shard_map(
        body,
        mesh=mesh,
        in_specs=(
            P(("gx", "gy"), None, None, None),
            P(("gx", "gy"), None, None, None, None),
            P(("gx", "gy"), None),
            P("gx", "gy", None),
            P("gx", "gy", None),
            P("gx", "gy"),
            P("gy", None, None, None, None),
        ),
        out_specs=P(("gx", "gy"), None, None, None),
        check_vma=False,
    )
```

```python
import jax
import jax.numpy as jnp
from jax import lax
from jax.experimental import pallas as pl
from jax.experimental.pallas import tpu as pltpu
from jax.sharding import PartitionSpec as P

MESH = pl.DeviceIdType.MESH
NT = (((1,), (1,)), ((), ()))
BF = jnp.bfloat16
F32 = jnp.float32
ZERO_SLOT = 512


def combine(z):
    z = z.reshape(z.shape[0] // 16, 2, 8, 256)
    re, im = z[:, 0], z[:, 1]
    out_re = re[:, :, :128] - im[:, :, 128:]
    out_im = im[:, :, :128] + re[:, :, 128:]
    return jnp.concatenate([out_re[:, None], out_im[:, None]], axis=1)


def kernel(
    dir_s, dir_v, src_v, kind_v, count_v, coef_hbm, table_hbm, tr_hbm,
    out,
    coef, table, tr, vc, send_own, recv_c, tx, recv_x, fw, ry_m, rz, pz, zk, lo, qz, plo,
    idx_v, idx_all, idx_s, list_v, list_s,
    sem_ld, sem_sm,
    cs, cr, xs, xr, ys, yr, zs, zr, is_, ir,
    zbs, zbr, ybs, ybr, cbs, cbr,
):
    z = lax.axis_index("gx")
    g = lax.axis_index("gy")
    c = lax.rem(g, 2)
    x = lax.rem(lax.div(g, 2), 4)
    y = lax.div(g, 8)
    xp = x + 1 - 2 * lax.rem(x, 2)
    xn = 3 - x
    xf = 3 - xp
    xh = lax.div(x, 2)
    oc = 1 - c

    def gid(yy, xx, cc):
        return (yy * 4 + xx) * 2 + cc

    dev_core = (z, gid(y, x, oc))
    dev_xp = (z, gid(y, xp, c))

    def yo(dy):
        return lax.rem(y + dy, 4)

    def zo(dz):
        return lax.rem(z + dz, 8)

    rel = (x, xp, xn, xf)

    def dev_n(n, dy):
        return (z, gid(yo(dy), rel[n], c))

    def dev_z(zz):
        return (zz, g)

    def rc(src, dst, ss, rs, dev):
        return pltpu.make_async_remote_copy(
            src_ref=src, dst_ref=dst, send_sem=ss, recv_sem=rs, device_id=dev, device_id_type=MESH
        )

    pend = []

    def go(cp):
        cp.start()
        pend.append(cp)

    def drain():
        for cp in pend:
            cp.wait_send()
        pend.clear()

    YS = (2, 1, 3)
    ZE = (4, 2, 6)
    ZO = (3, 5, 1, 7)
    ZR = (ZE, ZO)
    ZS = ZE + ZO
    pri = (xf, xp, xn, x)

    def slot(h):
        return lax.rem(z + h, 2)

    barrier = pltpu.get_barrier_semaphore()
    partners = [dev_core] + [dev_z(zo(dz)) for dz in ZS]
    partners += [dev_n(n, dy) for n in range(4) for dy in range(4) if n or dy]
    for dev in partners:
        pl.semaphore_signal(barrier, inc=1, device_id=dev, device_id_type=MESH)

    cp_coef = pltpu.make_async_copy(coef_hbm, coef, sem_ld.at[4])
    cp_coef.start()
    loads = []
    for k in range(4):
        cp = pltpu.make_async_copy(tr_hbm.at[:, :, pri[k]], tr.at[:, :, pri[k]], sem_ld.at[k])
        cp.start()
        loads.append(cp)

    cp_table = pltpu.make_async_copy(table_hbm, table, sem_ld.at[5])
    cp_table.start()

    for m in range(7):
        idx_v[2 * m : 2 * m + 2, 0:8] = jnp.where(
            count_v[...] > m, kind_v[m] * 64 + src_v[m], ZERO_SLOT
        )
    cp_coef.wait()

    def prep(n, carry):
        cc = lax.div(n, 16)
        i = lax.rem(n, 16)
        vt = coef[cc, i].astype(F32).T.reshape(2, 8, 8, 128)
        v = jnp.concatenate([vt[0][:, None], vt[1][:, None]], axis=1)
        vc[cc, i] = v.reshape(128, 128).astype(BF)
        return carry

    lax.fori_loop(0, 32, prep, 0, unroll=4)

    def up(d, k):
        def one(n, carry):
            yy = lax.rem(n, 4)
            first = lax.div(n, 4)
            cc = lax.rem(oc + first, 2)
            cd = cc * 2 + d
            e = yy * 16 + pri[k] * 4 + cd
            lhs = jnp.concatenate([vc[0, dir_s[0, e]], vc[1, dir_s[1, e]]], axis=1)
            rhs = jnp.concatenate(
                [tr[0, yy, pri[k], cd].reshape(256, 128), tr[1, yy, pri[k], cd].reshape(256, 128)], axis=1
            )
            r = combine(lax.dot_general(lhs, rhs, NT, preferred_element_type=F32))
            r = r.reshape(8, 16, 128).astype(BF)
            for h in range(2):
                send_own[d, slot(h), k, first, yy] = r[4 * h : 4 * h + 4]
            return carry

        lax.fori_loop(0, 8, one, 0, unroll=8)

    def core_copy(d, k):
        return rc(send_own.at[d, :, k, 0], recv_c.at[d, :, k], cs.at[d, k], cr.at[d, k], dev_core)

    def x_copy(d, r, k):
        return rc(tx.at[d, r, k], recv_x.at[d, r, k], xs.at[d, r, k], xr.at[d, r, k], dev_xp)

    def t_step(d, k):
        core_copy(d, k).wait_recv()
        for r in range(2):
            tx[d, r, k] = (send_own[d, r, k, 1].astype(F32) + recv_c[d, r, k].astype(F32)).astype(BF)
            go(x_copy(d, r, k))

    def add3(d, r, k):
        return (
            send_own[d, r, k + 2, 1].astype(F32)
            + recv_c[d, r, k + 2].astype(F32)
            + recv_x[d, r, k].astype(F32)
        ).astype(BF)

    def y_copy(d, r, n, dy, arrive):
        yy = yo(dy)
        yf = yy if arrive else y
        src = fw if n else ry_m
        p = yf * 2 + (1 - xh if n and arrive else xh)
        return rc(
            src.at[d, r, yy], rz.at[d, r, :, p], ys.at[d, r, n // 2, yy], yr.at[d, r, n // 2, yf], dev_n(n, dy)
        )

    def f_step(d, r):
        if r == 0:
            core_copy(d, 2).wait_recv()
        x_copy(d, r, 0).wait_recv()
        fw[d, r] = add3(d, r, 0)
        for dy in YS + (0,):
            go(y_copy(d, r, 2, dy, False))

    def g_step(d, r):
        if r == 0:
            core_copy(d, 3).wait_recv()
        x_copy(d, r, 1).wait_recv()
        ry_m[d, r] = add3(d, r, 1)
        for dy in YS:
            go(y_copy(d, r, 0, dy, False))
        rz[d, r, :, y * 2 + xh] = ry_m[d, r, y]

    def z_copy(d, dz, arrive):
        zz = zo(dz)
        zf = zz if arrive else z
        return rc(
            rz.at[d, dz % 2, lax.div(zz, 2)], pz.at[d, zf], zs.at[d, zz], zr.at[d, zf], dev_z(zz)
        )

    def z_send(d, r):
        for dy in YS + (0,):
            y_copy(d, r, 2, dy, True).wait_recv()
        for dy in YS:
            y_copy(d, r, 0, dy, True).wait_recv()
        for dz in ZR[r]:
            go(z_copy(d, dz, False))
        if r == 0:
            pz[d, z] = rz[d, 0, lax.div(z, 2)]

    def idx_copy(dz, arrive):
        zz = zo(dz)
        zf = zz if arrive else z
        return rc(idx_v, idx_all.at[zf], is_.at[zz], ir.at[zf], dev_z(zz))

    loads[0].wait()
    up(0, 0)
    pl.semaphore_wait(barrier, len(partners))
    go(core_copy(0, 0))
    loads[1].wait()
    up(0, 1)
    go(core_copy(0, 1))
    t_step(0, 0)
    loads[2].wait()
    up(0, 2)
    go(core_copy(0, 2))
    t_step(0, 1)
    for dz in ZS:
        go(idx_copy(dz, False))
    idx_all[z] = idx_v[...]
    loads[3].wait()
    up(0, 3)
    go(core_copy(0, 3))
    up(1, 0)
    go(core_copy(1, 0))
    f_step(0, 0)
    up(1, 1)
    go(core_copy(1, 1))
    f_step(0, 1)
    t_step(1, 0)
    up(1, 2)
    go(core_copy(1, 2))
    t_step(1, 1)
    g_step(0, 0)
    up(1, 3)
    go(core_copy(1, 3))
    g_step(0, 1)
    f_step(1, 0)

    lane = lax.broadcasted_iota(jnp.int32, (128, 128), 1)
    sub = lax.broadcasted_iota(jnp.int32, (128, 128), 0)
    for cc in range(2):
        list_v[cc : cc + 1, 0:64] = dir_v[cc : cc + 1, :]
        row = jnp.where(lane < 64, jnp.broadcast_to(list_v[cc : cc + 1, :], (128, 128)), 64)
        same = jnp.where((row == row.T) & (sub < lane), 1, 0)
        key = row * 4 + jnp.broadcast_to(jnp.sum(same, axis=0, keepdims=True), (128, 128))
        list_v[cc : cc + 1, :] = jnp.sum(jnp.where(key.T == lane, sub, 0), axis=0, keepdims=True)
    zk[ZERO_SLOT] = jnp.zeros((16, 128), F32)

    z_send(0, 0)
    f_step(1, 1)
    cp_list = pltpu.make_async_copy(list_v, list_s, sem_sm.at[0])
    cp_list.start()
    z_send(0, 1)
    g_step(1, 0)
    g_step(1, 1)
    cp_list.wait()
    for dz in ZS:
        idx_copy(dz, True).wait_recv()
    cp_idx = pltpu.make_async_copy(idx_all, idx_s, sem_sm.at[1])
    cp_idx.start()
    z_send(1, 0)
    cp_idx.wait()
    cp_table.wait()
    z_send(1, 1)

    def zb_copy(d, dz, arrive):
        zz = zo(dz)
        zf = zz if arrive else z
        return rc(
            lo.at[d, zz], qz.at[d, dz % 2, lax.div(zf, 2)], zbs.at[d, zz], zbr.at[d, zf], dev_z(zz)
        )

    def couple(d):
        for dz in ZS:
            z_copy(d, dz, True).wait_recv()

        def dense(k, carry):
            rhs = table[d, k].reshape(256, 128)
            for q in range(4):
                lhs = pz[d, q * 2 : q * 2 + 2].reshape(256, 128)
                r = combine(lax.dot_general(lhs, rhs, NT, preferred_element_type=F32))
                zk[pl.ds(k * 64 + q * 16, 16)] = r.reshape(16, 16, 128)
            return carry

        lax.fori_loop(0, 8, dense, 0, unroll=2)
        for dz in ZE + (0,) + ZO:
            zz = zo(dz)

            def row_sum(p, carry):
                acc = zk[idx_s[zz, d, p]]
                for m in range(1, 7):
                    acc = acc + zk[idx_s[zz, 2 * m + d, p]]
                lo[d, zz, p] = acc.astype(BF)
                return carry

            lax.fori_loop(0, 8, row_sum, 0, unroll=4)
            if dz:
                go(zb_copy(d, dz, False))
        qz[d, 0, lax.div(z, 2)] = lo[d, z]

    NS = (3, 2, 1, 0)

    def yb_copy(d, r, n, dy, arrive):
        yy = yo(dy)
        yf, xs_ = (yy, rel[n]) if arrive else (y, x)
        p = yy * 2 + (xh if n < 2 else 1 - xh)
        return rc(
            qz.at[d, r, :, p], plo.at[r, yf, xs_, c * 2 + d],
            ybs.at[d, r, n, yy], ybr.at[d, r, n, yf], dev_n(n, dy),
        )

    def yb_step(d, r):
        for dz in ZR[r]:
            zb_copy(d, dz, True).wait_recv()
        for n in NS:
            for dy in YS + (0,):
                if n or dy:
                    go(yb_copy(d, r, n, dy, False))
        plo[r, y, x, c * 2 + d] = qz[d, r, :, y * 2 + xh]

    def grp(r, xx, cc, d):
        return plo.at[r, :, xx, cc * 2 + d]


    def cb_copy(d, r, n, cc):
        ref = grp(r, rel[n], cc, d)
        return rc(ref, ref, cbs.at[d, r, n], cbr.at[d, r, n], dev_core)

    def xb_step(d, r):
        for n in (0, 1, 2, 3):
            for dy in YS + (0,):
                if n or dy:
                    yb_copy(d, r, n, dy, True).wait_recv()
            go(cb_copy(d, r, n, c))

    couple(0)
    couple(1)
    yb_step(0, 0)
    yb_step(0, 1)
    xb_step(0, 0)
    yb_step(1, 0)
    xb_step(0, 1)
    yb_step(1, 1)
    xb_step(1, 0)
    drain()
    xb_step(1, 1)
    for d in range(2):
        for r in range(2):
            for n in range(4):
                cb_copy(d, r, n, oc).wait_recv()

    drain()

    def down(n, carry):
        cc = lax.div(n, 16)
        i = lax.rem(n, 16)
        lhs, rhs = [], []
        for j in range(4):
            e = list_s[cc, i * 4 + j]
            ey = lax.div(e, 16)
            ex = lax.rem(lax.div(e, 4), 4)
            ec = lax.rem(e, 4)
            halves = [plo[slot(h), ey, ex, ec].reshape(64, 128) for h in range(2)]
            lhs.append(jnp.concatenate(halves, axis=0))
            m = tr[cc, ey, ex, ec]
            rhs.append(jnp.concatenate([m[0], m[1]], axis=1))
        r = combine(
            jnp.dot(
                jnp.concatenate(lhs, axis=1), jnp.concatenate(rhs, axis=0), preferred_element_type=F32
            )
        )
        t = jnp.concatenate([r[:, 0].reshape(64, 128), r[:, 1].reshape(64, 128)], axis=0)
        out[cc, i] = t.T.astype(BF)
        return carry

    lax.fori_loop(0, 32, down, 0, unroll=8)


def body(child_coef, transfer, child_dir, couple_src, couple_kind, couple_count, couple_table):
    flip = (2, 1, 0)
    src, kind = couple_src.transpose(flip), couple_kind.transpose(flip)
    tr = transfer.reshape(2, 4, 4, 4, 2, 128, 128)
    vm = pl.BlockSpec(memory_space=pltpu.VMEM)
    hbm = pl.BlockSpec(memory_space=pl.ANY)
    dma = pltpu.SemaphoreType.DMA

    def blk(*lead):
        return pltpu.VMEM(lead + (4, 16, 128), BF)

    return pl.pallas_call(
        kernel,
        out_shape=pltpu.VMEM((2, 16, 128, 128), BF),
        in_specs=[pl.BlockSpec(memory_space=pltpu.SMEM), vm, vm, vm, vm, hbm, hbm, hbm],
        out_specs=vm,
        scratch_shapes=[
            pltpu.VMEM((2, 16, 128, 128), BF),
            pltpu.VMEM((2, 8, 2, 128, 128), BF),
            pltpu.VMEM((2, 4, 4, 4, 2, 128, 128), BF),
            pltpu.VMEM((2, 16, 128, 128), BF),
            blk(2, 2, 4, 2, 4),
            blk(2, 2, 4, 4),
            blk(2, 2, 2, 4),
            blk(2, 2, 2, 4),
            blk(2, 2, 4),
            blk(2, 2, 4),
            pltpu.VMEM((2, 2, 4, 8, 16, 128), BF),
            pltpu.VMEM((2, 8, 8, 16, 128), BF),
            pltpu.VMEM((ZERO_SLOT + 1, 16, 128), F32),
            pltpu.VMEM((2, 8, 8, 16, 128), BF),
            pltpu.VMEM((2, 2, 4, 8, 16, 128), BF),
            blk(2, 4, 4, 4),
            pltpu.VMEM((16, 128), jnp.int32),
            pltpu.VMEM((8, 16, 128), jnp.int32),
            pltpu.SMEM((8, 16, 128), jnp.int32),
            pltpu.VMEM((8, 128), jnp.int32),
            pltpu.SMEM((8, 128), jnp.int32),
            dma((6,)), dma((2,)),
            dma((2, 4)), dma((2, 4)),
            dma((2, 2, 2)), dma((2, 2, 2)),
            dma((2, 2, 2, 4)), dma((2, 2, 2, 4)),
            dma((2, 8)), dma((2, 8)),
            dma((8,)), dma((8,)),
            dma((2, 8)), dma((2, 8)),
            dma((2, 2, 4, 4)), dma((2, 2, 4, 4)),
            dma((2, 2, 4)), dma((2, 2, 4)),
        ],
        compiler_params=pltpu.CompilerParams(
            collective_id=0, has_side_effects=True, vmem_limit_bytes=56 * 1024 * 1024
        ),
        name="h2_pass",
    )(child_dir, child_dir, src, kind, couple_count.T, child_coef, couple_table, tr)


def solution(mesh):
    return jax.shard_map(
        body,
        mesh=mesh,
        in_specs=(
            P(("gx", "gy"), None, None, None),
            P(("gx", "gy"), None, None, None, None),
            P(("gx", "gy"), None),
            P("gx", "gy", None),
            P("gx", "gy", None),
            P("gx", "gy"),
            P("gy", None, None, None, None),
        ),
        out_specs=P(("gx", "gy"), None, None, None),
        check_vma=False,
    )
```
